32 devices in a mesh: row: 8 (over z, core), col: 4 (over y, x).
Axes of the slice: x: 2, y: 2, z: 4, core: 2. Of those that a mesh axis runs over, the one named last changes fastest.
Arguments:
- source: float32 [16, 256, 512], P(None, 'row', 'col'), may hold values from -6 to 6
- guess: float32 [16, 256, 512], P(None, 'row', 'col'), may hold values from -6 to 6
- conductivity: float32 [256, 512], P('row', 'col'), may hold values from 0.1 to 10
- storage: float32 [256, 512], P('row', 'col'), may hold values from 0.02 to 0.2
- aggregates: int32 [256, 512], P('row', 'col'), may hold values from 0 to 63, as said below
- pair_maps: int32 [4, 8, 4, 128], P(None, 'row', 'col'), may hold values from 0 to 63, as said below
Outputs:
- solution: float32 [16, 256, 512], P(None, 'row', 'col')
- residual: float32 [16, 256, 512], P(None, 'row', 'col')
The draws below stay inside these ranges and needn't reach their ends.
Inputs may be any that keep to these rules, and one draw needn't show every extreme that they name: `aggregates`: within each tile of 32 x 128 cells every id from 0 to 63 names exactly 64 cells of that tile. pair_maps[k, r, c] is the same for all tiles of one group of agglomeration level k + 1, that is all tiles whose row index shifted right by (k + 1) // 2 bits and column index shifted right by (k + 2) // 2 bits agree; each coarse unknown receives exactly two of the 128 entries.
All inputs are finite; a program needn't handle non-finite values.
Results may differ from the reference program's by a relative error of at most 0.0003.
Values sent between devices are 32-bit elements; how exact they have to be, the bound alone decides.
A program may use at most 64 MiB of HBM per device.

```python
import math
import jax
import jax.numpy as jnp
from jax import lax

CY = 32
CX = 128
NA = 64
M = 16
SWEEPS = 3
LEVELS = 4
NY = 256
NX = 512
N_ROW = 8
N_COL = 4


def draw_aggregates(key, part):
    rows_tiles = NY // CY
    cols_tiles = NX // CX
    key_shift, key_perm = jax.random.split(key)
    shifts = jax.random.randint(key_shift, (NY, cols_tiles), 0, 8)
    row_pos = jnp.arange(NY, dtype=jnp.int32)[:, None]
    col_pos = jnp.arange(NX, dtype=jnp.int32)[None, :]
    tile_col = col_pos // CX
    shift_cell = jnp.take(shifts, tile_col[0], axis=1)
    local_row = row_pos % CY
    local_col = col_pos % CX
    block_id = local_row // 8 * (CX // 8) + (local_col + shift_cell) % CX // 8
    perm_keys = jax.random.split(key_perm, rows_tiles * cols_tiles)
    labels = jax.vmap(lambda single: jax.random.permutation(single, NA))(perm_keys)
    tile_id = row_pos // CY * cols_tiles + tile_col
    return labels[tile_id, block_id].astype(jnp.int32)


def draw_pair_maps(key, part):
    rows_tiles = NY // CY
    cols_tiles = NX // CX
    keys = jax.random.split(key, LEVELS * rows_tiles * cols_tiles)
    perms = jax.vmap(lambda single: jax.random.permutation(single, 2 * NA))(keys)
    perms = perms.reshape(LEVELS, rows_tiles, cols_tiles, 2 * NA)
    result = []
    for level in range(LEVELS):
        row_bits = (level + 1) // 2
        col_bits = (level + 2) // 2
        rep_rows = jnp.arange(rows_tiles, dtype=jnp.int32) >> row_bits << row_bits
        rep_cols = jnp.arange(cols_tiles, dtype=jnp.int32) >> col_bits << col_bits
        chosen = perms[level][rep_rows[:, None], rep_cols[None, :]]
        result.append(chosen // 2)
    return jnp.stack(result).astype(jnp.int32)


def steps_of(rng, dims, cuts, smallest, high):
    factor_of, own = 1.0, jax.random.fold_in(rng, 6)
    for position, shards_of in cuts:
        draws = jnp.exp(jax.random.uniform(jax.random.fold_in(own, position), (shards_of,), jnp.float32, smallest / len(cuts), high / len(cuts)))
        factor_of = factor_of * jnp.repeat(draws, dims[position] // shards_of).reshape([-1 if axis == position else 1 for axis in range(len(dims))])
    return factor_of


def gaussian(rng, extent, spread, most, cuts=(), kind=jnp.bfloat16):
    array = jax.random.normal(rng, extent, jnp.float32) * spread
    if len(cuts) > 0:
        array = steps_of(rng, extent, cuts, -0.22, 0.18) * array
    return jnp.clip(array, min=-most, max=most).astype(kind)


def setup_inputs(seed: int = 0) -> dict:
    seeds = jax.random.split(jax.random.key(seed), 7)
    source = gaussian(seeds[0], (M, NY, NX), 1.0, 6.0, ((1, 8), (2, 4)), jnp.float32)
    guess = gaussian(seeds[1], (M, NY, NX), 1.0, 6.0, ((1, 8), (2, 4)), jnp.float32)
    conductivity = jnp.clip(jnp.exp(math.log(10.0) - 4.6051702 * jax.random.uniform(seeds[2], (NY, NX), jnp.float32) ** steps_of(seeds[2], (NY, NX), ((0, 8), (1, 4)), -0.2, 0.2)), 0.1, 10.0)
    storage = jnp.clip(jnp.exp(math.log(0.2) - 2.3025851 * jax.random.uniform(seeds[3], (NY, NX), jnp.float32) ** steps_of(seeds[3], (NY, NX), ((0, 8), (1, 4)), -0.2, 0.2)), 0.02, 0.2)
    aggregates = draw_aggregates(jax.random.fold_in(seeds[6], 71), 0)
    pair_maps = draw_pair_maps(jax.random.fold_in(seeds[6], 71), 0)
    return {"source": source, "guess": guess, "conductivity": conductivity, "storage": storage, "aggregates": aggregates, "pair_maps": pair_maps}


OMEGA_FINE = 0.8
OMEGA_COARSE = 0.6
HIGHEST = lax.Precision.HIGHEST

def face_values(cond):
    across = 2.0 * (cond[:, :-1] * cond[:, 1:]) / (cond[:, :-1] + cond[:, 1:])
    downward = 2.0 * (cond[:-1, :] * cond[1:, :]) / (cond[:-1, :] + cond[1:, :])
    east_face = jnp.pad(across, ((0, 0), (0, 1)))
    west_face = jnp.pad(across, ((0, 0), (1, 0)))
    south_face = jnp.pad(downward, ((0, 1), (0, 0)))
    north_face = jnp.pad(downward, ((1, 0), (0, 0)))
    return (east_face, west_face, south_face, north_face)

def mat_apply(vector, matrix):
    return jnp.matmul(vector, jnp.swapaxes(matrix, -1, -2), precision=HIGHEST)

def presmooth(rhs, apply_fn, diag_row):
    approx = OMEGA_COARSE * rhs / diag_row
    for sweep_index in range(SWEEPS - 1):
        approx = approx + OMEGA_COARSE * (rhs - apply_fn(approx)) / diag_row
    return approx

def postsmooth(rhs, approx, apply_fn, diag_row):
    for sweep_index in range(SWEEPS):
        approx = approx + OMEGA_COARSE * (rhs - apply_fn(approx)) / diag_row
    return approx

def solve_block(matrix, rhs):
    factor = jnp.linalg.cholesky(matrix)
    return jax.scipy.linalg.cho_solve((factor, True), rhs.T).T

def reference(source, guess, conductivity, storage, aggregates, pair_maps):
    east_face, west_face, south_face, north_face = face_values(conductivity)
    diagonal = storage + east_face + west_face + south_face + north_face

    def apply_fine(field):
        padded = jnp.pad(field, ((0, 0), (1, 1), (1, 1)))
        beside = east_face * padded[:, 1:-1, 2:] + west_face * padded[:, 1:-1, :-2] + south_face * padded[:, 2:, 1:-1] + north_face * padded[:, :-2, 1:-1]
        return diagonal * field - beside
    row_pos = jnp.arange(NY, dtype=jnp.int32)[:, None]
    col_pos = jnp.arange(NX, dtype=jnp.int32)[None, :]
    tile_id = row_pos // CY * N_COL + col_pos // CX
    base = tile_id * NA
    cell_key = (base + aggregates).reshape(-1)
    segments = N_ROW * N_COL * NA

    def restrict_all(field):
        summed = jax.ops.segment_sum(field.reshape(M, -1).T, cell_key, num_segments=segments)
        return summed.reshape(N_ROW, N_COL, NA, M).transpose(0, 1, 3, 2)

    def prolong_all(coarse):
        flat = coarse.transpose(2, 0, 1, 3).reshape(M, -1)
        return flat[:, cell_key].reshape(M, NY, NX)

    def level_one(coarse):
        return restrict_all(apply_fine(prolong_all(coarse)))
    right_agg = jnp.concatenate([aggregates[:, 1:], aggregates[:, :1]], axis=1)
    below_agg = jnp.concatenate([aggregates[1:, :], aggregates[:1, :]], axis=0)
    inner_east = jnp.where(col_pos % CX < CX - 1, east_face, 0.0)
    inner_south = jnp.where(row_pos % CY < CY - 1, south_face, 0.0)
    keys = jnp.concatenate([((base + aggregates) * NA + right_agg).reshape(-1), ((base + right_agg) * NA + aggregates).reshape(-1), ((base + aggregates) * NA + below_agg).reshape(-1), ((base + below_agg) * NA + aggregates).reshape(-1), ((base + aggregates) * NA + aggregates).reshape(-1)])
    values = jnp.concatenate([(-inner_east).reshape(-1), (-inner_east).reshape(-1), (-inner_south).reshape(-1), (-inner_south).reshape(-1), diagonal.reshape(-1)])
    self_block = jax.ops.segment_sum(values, keys, num_segments=N_ROW * N_COL * NA * NA).reshape(N_ROW, N_COL, NA, NA)
    solution = guess
    for sweep_index in range(SWEEPS):
        solution = solution + OMEGA_FINE * (source - apply_fine(solution)) / diagonal
    leftover = source - apply_fine(solution)
    rhs_list = [restrict_all(leftover)]
    mat_list = [self_block]
    diag_one = jnp.diagonal(self_block, axis1=-2, axis2=-1)[..., None, :]
    sol_list = [presmooth(rhs_list[0], level_one, diag_one)]
    remainder = rhs_list[0] - level_one(sol_list[0])
    own_maps = []
    labels = jnp.arange(NA, dtype=jnp.int32)
    for level in range(LEVELS):
        axis_num = 1 if level % 2 == 0 else 0
        bit = level // 2
        count = N_COL if axis_num == 1 else N_ROW
        positions = jnp.arange(count, dtype=jnp.int32)
        upper_bit = positions >> bit & 1
        lower_pos = positions - upper_bit * (1 << bit)
        upper_pos = lower_pos + (1 << bit)
        mat_lo = jnp.take(mat_list[-1], lower_pos, axis=axis_num)
        mat_hi = jnp.take(mat_list[-1], upper_pos, axis=axis_num)
        rhs_lo = jnp.take(remainder, lower_pos, axis=axis_num)
        rhs_hi = jnp.take(remainder, upper_pos, axis=axis_num)
        if axis_num == 1:
            flags = upper_bit[None, :, None, None]
        else:
            flags = upper_bit[:, None, None, None]
        chooser = (pair_maps[level][..., None] == labels).astype(jnp.float32)
        q_lo = chooser[..., :NA, :]
        q_hi = chooser[..., NA:, :]
        coarse_mat = jnp.matmul(jnp.swapaxes(q_lo, -1, -2), jnp.matmul(mat_lo, q_lo, precision=HIGHEST), precision=HIGHEST) + jnp.matmul(jnp.swapaxes(q_hi, -1, -2), jnp.matmul(mat_hi, q_hi, precision=HIGHEST), precision=HIGHEST)
        coarse_rhs = jnp.matmul(rhs_lo, q_lo, precision=HIGHEST) + jnp.matmul(rhs_hi, q_hi, precision=HIGHEST)
        own_maps.append(jnp.where(flags == 1, q_hi, q_lo))
        mat_list.append(coarse_mat)
        rhs_list.append(coarse_rhs)
        if level < LEVELS - 1:
            diag_row = jnp.diagonal(coarse_mat, axis1=-2, axis2=-1)[..., None, :]
            approx = presmooth(coarse_rhs, lambda vec, mat=coarse_mat: mat_apply(vec, mat), diag_row)
            remainder = coarse_rhs - mat_apply(approx, coarse_mat)
        else:
            flat = jax.vmap(solve_block)(coarse_mat.reshape(-1, NA, NA), coarse_rhs.reshape(-1, M, NA))
            approx = flat.reshape(N_ROW, N_COL, M, NA)
        sol_list.append(approx)
    for level in reversed(range(LEVELS)):
        updated = sol_list[level] + mat_apply(sol_list[level + 1], own_maps[level])
        if level > 0:
            matrix = mat_list[level]
            diag_row = jnp.diagonal(matrix, axis1=-2, axis2=-1)[..., None, :]
            updated = postsmooth(rhs_list[level], updated, lambda vec, mat=matrix: mat_apply(vec, mat), diag_row)
        else:
            updated = postsmooth(rhs_list[0], updated, level_one, diag_one)
        sol_list[level] = updated
    solution = solution + prolong_all(sol_list[0])
    for sweep_index in range(SWEEPS):
        solution = solution + OMEGA_FINE * (source - apply_fine(solution)) / diagonal
    residual = source - apply_fine(solution)
    return (solution, residual)
```

```python
import functools

import jax
import jax.numpy as jnp
from jax import lax
from jax.experimental import pallas as pl
from jax.experimental.pallas import tpu as pltpu
from jax.sharding import PartitionSpec as P

NA = 64
SWEEPS = 3
LEVELS = 4
OMEGA_FINE = 0.8
OMEGA_COARSE = 0.6
F32 = jnp.float32
BF16 = jnp.bfloat16
MESH = pl.DeviceIdType.MESH
OPP = (1, 0, 3, 2)
NU = 2 * (SWEEPS + 1)
NX0 = 2 * SWEEPS
NN = (((1,), (0,)), ((), ()))
NT = (((1,), (1,)), ((), ()))


def dg(a, b, dims):
    return lax.dot_general(a, b, dims, preferred_element_type=F32)


def split2(x):
    hi = x.astype(BF16)
    return hi, (x - hi.astype(F32)).astype(BF16)


def split3(x):
    hi = x.astype(BF16)
    rest = x - hi.astype(F32)
    mid = rest.astype(BF16)
    return hi, mid, (rest - mid.astype(F32)).astype(BF16)


def dot_parts(x, w_hi, w_lo):
    hi, lo = split2(x)
    return dg(hi, w_hi, NN) + (dg(lo, w_hi, NN) + dg(hi, w_lo, NN))


def dot_hot(x, hot, dims):
    hi, mid, lo = split3(x)
    return dg(hi, hot, dims) + (dg(mid, hot, dims) + dg(lo, hot, dims))


def hot_dot(hot, x, dims):
    hi, mid, lo = split3(x)
    return dg(hot, hi, dims) + (dg(hot, mid, dims) + dg(hot, lo, dims))


def kernel(n_row, n_col, src, guess, cond, sto, agg, pm, sol, res,
           u, left, mo, gmat, rlhs, xt, crecv, arecv, rowbuf, colbuf, rsend, csend,
           xsend, xrecv, msend, mrecv, vsend, vrecv, wmat, bsp, qts, ssem, rsem):
    members, rows, cols = guess.shape
    row = lax.axis_index("row")
    col = lax.axis_index("col")
    has = (row > 0, row < n_row - 1, col > 0, col < n_col - 1)
    dev = ((row - 1, col), (row + 1, col), (row, col - 1), (row, col + 1))
    col_bit = col % 2
    row_bit = row % 2
    col_bit2 = col // 2 % 2
    row_bit2 = row // 2 % 2
    upper = (col_bit, row_bit, col_bit2, row_bit2)
    partner = (
        (row, col + 1 - 2 * col_bit),
        (row + 1 - 2 * row_bit, col),
        (row, col + 2 - 4 * col_bit2),
        (row + 2 - 4 * row_bit2, col),
    )

    barrier = pltpu.get_barrier_semaphore()
    count = jnp.int32(2)
    for d in range(4):
        count = count + has[d].astype(jnp.int32)

        @pl.when(has[d])
        def _():
            pl.semaphore_signal(barrier, inc=1, device_id=dev[d], device_id_type=MESH)

    for k in (2, 3):
        pl.semaphore_signal(barrier, inc=1, device_id=partner[k], device_id_type=MESH)

    def copy(source, target, slot, device):
        return pltpu.make_async_remote_copy(
            src_ref=source, dst_ref=target, send_sem=ssem.at[slot], recv_sem=rsem.at[slot],
            device_id=device, device_id_type=MESH)

    sent = []

    def start(d, source, target, slot):
        @pl.when(has[d])
        def _():
            copy(source, target, slot, dev[d]).start()

        sent.append((d, source, target, slot))

    def arrive(d, source, target, slot):
        @pl.when(has[OPP[d]])
        def _():
            copy(source, target, slot, dev[d]).wait_recv()

    for d in range(4):
        @pl.when(jnp.logical_not(has[OPP[d]]))
        def _():
            crecv[d] = jnp.ones((rows, cols), F32)
            arecv[d] = jnp.zeros((rows, cols), jnp.int32)
            for e in range(NU):
                if d < 2:
                    rowbuf[e, d] = jnp.zeros((members, cols), F32)
                else:
                    colbuf[e, d - 2] = jnp.zeros((rows, cols), F32)
            for e in range(NX0):
                xrecv[e, d] = jnp.zeros((members, cols), F32)

    lane = lax.broadcasted_iota(jnp.int32, (rows, cols), 1)
    sub = lax.broadcasted_iota(jnp.int32, (rows, cols), 0)
    pair_lane = lane // 2

    def u_sources(e):
        return (rsend.at[e, 0], rsend.at[e, 1], csend.at[e], csend.at[e])

    def u_targets(e):
        return (rowbuf.at[e, 0], rowbuf.at[e, 1], colbuf.at[e, 0], colbuf.at[e, 1])

    def pack(e, field_of):
        packed = jnp.zeros((rows, cols), F32)
        for m in range(members):
            v = field_of(m)
            packed = jnp.where(pair_lane == m, pltpu.roll(v, 2 * m + 1, 1), packed)
            rsend[e, 0, m : m + 1, :] = v[0:1]
            rsend[e, 1, m : m + 1, :] = v[rows - 1 : rows]
        csend[e] = packed

    def u_start(e):
        for d in (2, 3, 0, 1):
            start(d, u_sources(e)[d], u_targets(e)[d], 8 + 4 * e + d)

    def u_arrive(e):
        for d in range(4):
            arrive(d, u_sources(e)[d], u_targets(e)[d], 8 + 4 * e + d)

    pack(0, lambda m: guess[m])
    pl.semaphore_wait(barrier, count)
    for d in range(4):
        start(d, cond, crecv.at[d], d)
        start(d, agg, arecv.at[d], 4 + d)
    u_start(0)

    agg_v = agg[...]
    sub64 = lax.broadcasted_iota(jnp.int32, (NA, cols), 0)
    for r in range(rows):
        mo[:, r * cols : (r + 1) * cols] = jnp.where(
            sub64 == agg_v[r : r + 1], 1.0, 0.0).astype(BF16)
    wmat[...] = jnp.zeros(wmat.shape, BF16)
    msend[...] = jnp.zeros(msend.shape, F32)
    xt[...] = jnp.zeros(xt.shape, F32)
    iota128 = lax.broadcasted_iota(jnp.int32, (cols, cols), 0)
    for k in range(LEVELS):
        pmk = pm[k : k + 1, :]
        pmk = jnp.where(upper[k] == 1, pltpu.roll(pmk, NA, 1), pmk)
        qts[k] = jnp.where(iota128 == pmk, 1.0, 0.0).astype(BF16)

    for d in range(4):
        arrive(d, cond, crecv.at[d], d)
        arrive(d, agg, arecv.at[d], 4 + d)
    c = cond[...]

    def face(other):
        return 2.0 * (c * other) / (c + other)

    last = rows - 1
    east = face(jnp.where(lane == cols - 1, pltpu.roll(crecv[2], cols - 1, 1), pltpu.roll(c, cols - 1, 1)))
    west = face(jnp.where(lane == 0, pltpu.roll(crecv[3], 1, 1), pltpu.roll(c, 1, 1)))
    south = face(jnp.where(sub == last, pltpu.roll(crecv[0], last, 0), pltpu.roll(c, last, 0)))
    north = face(jnp.where(sub == 0, pltpu.roll(crecv[1], 1, 0), pltpu.roll(c, 1, 0)))
    hasi = [h.astype(jnp.int32) for h in has]
    north = jnp.where(sub >= 1 - hasi[0], north, 0.0)
    south = jnp.where(sub < last + hasi[1], south, 0.0)
    west = jnp.where(lane >= 1 - hasi[2], west, 0.0)
    east = jnp.where(lane < cols - 1 + hasi[3], east, 0.0)
    diag = sto[...] + east + west + south + north
    step = OMEGA_FINE / diag

    def apply_field(e, finish):
        h_in = jnp.where(lane % 2 == 0, colbuf[e, 1], pltpu.roll(colbuf[e, 0], cols - 2, 1))
        for m in range(members):
            v = u[m]
            hm = pltpu.roll(h_in, (cols - 2 * m) % cols, 1)
            from_w = jnp.where(lane == 0, hm, pltpu.roll(v, 1, 1))
            from_e = jnp.where(lane == cols - 1, hm, pltpu.roll(v, cols - 1, 1))
            from_s = jnp.where(sub == last, rowbuf[e, 0, m : m + 1, :], pltpu.roll(v, last, 0))
            from_n = jnp.where(sub == 0, rowbuf[e, 1, m : m + 1, :], pltpu.roll(v, 1, 0))
            rest = src[m] - (diag * v - (east * from_e + west * from_w + south * from_s + north * from_n))
            finish(m, v, rest)

    def sweep(e):
        def finish(m, v, rest):
            u[m] = v + step * rest

        apply_field(e, finish)
        pack(e + 1, lambda m: u[m])
        u_start(e + 1)

    in_east = jnp.where(lane < cols - 1, east, 0.0)
    in_south = jnp.where(sub < last, south, 0.0)
    right = pltpu.roll(agg_v, cols - 1, 1)
    below = pltpu.roll(agg_v, last, 0)
    half = 0.5 * diag
    for r in range(rows):
        s = slice(r, r + 1)
        g = (jnp.where(sub64 == right[s], in_east[s], 0.0)
             + jnp.where(sub64 == below[s], in_south[s], 0.0)
             - jnp.where(sub64 == agg_v[s], half[s], 0.0))
        for i, part in enumerate(split3(g)):
            gmat[i * NA : (i + 1) * NA, r * cols : (r + 1) * cols] = part
    gx = dg(gmat[...], mo[...], NT)
    xt[0:NA, 0:NA] = gx[0:NA] + (gx[NA : 2 * NA] + gx[2 * NA : 3 * NA])
    xfull = xt[...]
    block = -(xfull + xfull.T)[0:NA]
    msend[0] = block

    def mat_copy(k):
        return copy(msend.at[k], mrecv.at[k], 8 + 4 * (NU + NX0) + k, partner[k])

    def vec_copy(k):
        return copy(vsend.at[k], vrecv.at[k], 8 + 4 * (NU + NX0) + LEVELS + k, partner[k])

    mat_copy(0).start()

    lane_c = lax.broadcasted_iota(jnp.int32, (NA, cols), 1)
    lane_1 = lax.broadcasted_iota(jnp.int32, (1, cols), 1)

    def weight(mat):
        d = jnp.sum(jnp.where(lane_c == sub64, mat, 0.0), axis=0, keepdims=True)
        ok = lane_1 < NA
        return jnp.where(ok, OMEGA_COARSE / jnp.where(ok, d, 1.0), 0.0)

    weights = [weight(block)]

    def next_mat(k):
        mat_copy(k).wait_recv()
        both = jnp.concatenate([msend[k], pltpu.roll(mrecv[k], NA, 1)], axis=0)
        qt = qts[k]
        mat = hot_dot(qt[0:NA], dot_hot(both, qt, NT), NN)
        msend[k + 1] = mat
        if k + 1 < LEVELS:
            mat_copy(k + 1).start()
            hi, lo = split2(mat)
            bsp[k, 0] = hi
            bsp[k, 1] = lo
            weights.append(weight(mat))

    u[...] = guess[...]
    u_arrive(0)
    sweep(0)

    agg_t = agg_v.astype(F32).T.astype(jnp.int32)

    def couple(slot, own_ids, other_ids, faces, width):
        own = jnp.where(lax.broadcasted_iota(jnp.int32, (cols, width), 0) == own_ids, 1.0, 0.0).astype(BF16)
        other = jnp.where(lax.broadcasted_iota(jnp.int32, (NA, width), 0) == other_ids, faces, 0.0)
        hi, lo = split2(-dot_hot(other, own, NT))
        wmat[0, slot * cols : slot * cols + NA] = hi
        wmat[1, slot * cols : slot * cols + NA] = lo

    hi, lo = split2(block)
    wmat[0, 0:NA] = hi
    wmat[1, 0:NA] = lo
    couple(1, agg_v[last : rows], arecv[0][0:1], south[last : rows], cols)
    couple(2, agg_v[0:1], arecv[1][last : rows], north[0:1], cols)
    agg_e = arecv[2].astype(F32).T.astype(jnp.int32)
    agg_w = arecv[3].astype(F32).T.astype(jnp.int32)
    couple(3, agg_t[cols - 1 : cols], agg_e[0:1], east.T[cols - 1 : cols], rows)
    couple(4, agg_t[0:1], agg_w[cols - 1 : cols], west.T[0:1], rows)
    next_mat(0)
    u_arrive(1)
    sweep(1)
    next_mat(1)
    u_arrive(2)
    sweep(2)
    next_mat(2)
    u_arrive(3)

    def keep_left(m, v, rest):
        left[m] = rest

    apply_field(3, keep_left)
    for r in range(rows):
        for i, part in enumerate(split3(left[:, r, :])):
            rlhs[i * members : (i + 1) * members, r * cols : (r + 1) * cols] = part
    gr = dg(rlhs[...], mo[...], NT)
    vsend[LEVELS] = jnp.zeros((members, cols), F32)
    vsend[LEVELS, :, 0:NA] = gr[0:members] + (gr[members : 2 * members] + gr[2 * members : 3 * members])
    y0 = vsend[LEVELS]

    def x_slot(e, d):
        return (d, xsend.at[e], xrecv.at[e, d], 8 + 4 * NU + 4 * e + d)

    def level_one(e, x, between=None):
        xsend[e] = x
        for d in (2, 3, 0, 1):
            start(*x_slot(e, d))
        if between is not None:
            between()
        for d in range(4):
            arrive(*x_slot(e, d))
        every = jnp.concatenate([x] + [xrecv[e, d] for d in range(4)], axis=1)
        return dot_parts(every, wmat[0], wmat[1])

    inverse = []

    def last_mat():
        next_mat(3)
        mat = jnp.where(lane_c < NA, msend[LEVELS], jnp.where(lane_c - NA == sub64, 1.0, 0.0))
        for k in range(NA):
            pivot = mat[k : k + 1] / mat[k : k + 1, k : k + 1]
            mat = jnp.where(sub64 == k, pivot, mat - mat[:, k : k + 1] * pivot)
        inverse.append(jnp.where(lane_c < NA, pltpu.roll(mat, NA, 1), 0.0))

    x = y0 * weights[0]
    x = x + (y0 - level_one(0, x, last_mat)) * weights[0]
    x = x + (y0 - level_one(1, x)) * weights[0]
    rem = y0 - level_one(2, x)
    sols, rhss = [x], [y0]
    for k in range(LEVELS):
        vsend[k] = rem
        vec_copy(k).start()
        vec_copy(k).wait_recv()
        y = dot_hot(rem + pltpu.roll(vrecv[k], NA, 1), qts[k], NT)
        rhss.append(y)
        if k < LEVELS - 1:
            apply_c = lambda z: dot_parts(z[:, 0:NA], bsp[k, 0], bsp[k, 1])
            w = weights[k + 1]
            x = y * w
            for _ in range(SWEEPS - 1):
                x = x + (y - apply_c(x)) * w
            rem = y - apply_c(x)
        else:
            x = lax.dot_general(y[:, 0:NA], inverse[0], NN, precision=lax.Precision.HIGHEST,
                                preferred_element_type=F32)
        sols.append(x)
    lane_m = lax.broadcasted_iota(jnp.int32, (members, cols), 1)
    for k in reversed(range(LEVELS)):
        x = sols[k] + jnp.where(lane_m < NA, dot_hot(x, qts[k], NN), 0.0)
        for i in range(SWEEPS):
            if k > 0:
                applied = dot_parts(x[:, 0:NA], bsp[k - 1, 0], bsp[k - 1, 1])
            else:
                applied = level_one(SWEEPS + i, x)
            x = x + (rhss[k] - applied) * weights[k]

    for r in range(rows):
        part = dot_hot(x[:, 0:NA], mo[:, r * cols : (r + 1) * cols], NN)
        u[:, r, :] = u[:, r, :] + part
    first = SWEEPS + 1
    pack(first, lambda m: u[m])
    u_start(first)
    for i in range(SWEEPS):
        u_arrive(first + i)
        sweep(first + i)
    u_arrive(first + SWEEPS)

    def out(m, v, rest):
        sol[m] = v
        res[m] = rest

    apply_field(first + SWEEPS, out)
    for d, source, target, slot in sent:
        @pl.when(has[d])
        def _():
            copy(source, target, slot, dev[d]).wait_send()

    for k in range(LEVELS):
        mat_copy(k).wait_send()
        vec_copy(k).wait_send()


def shards(n_row, n_col, source, guess, conductivity, storage, aggregates, pair_maps):
    members, rows, cols = source.shape
    cells = rows * cols
    vm = pl.BlockSpec(memory_space=pltpu.VMEM)
    slots = 8 + 4 * (NU + NX0) + 2 * LEVELS
    return pl.pallas_call(
        functools.partial(kernel, n_row, n_col),
        out_shape=(jax.ShapeDtypeStruct(source.shape, F32),) * 2,
        in_specs=[vm] * 6,
        out_specs=(vm, vm),
        scratch_shapes=[
            pltpu.VMEM((members, rows, cols), F32),
            pltpu.VMEM((members, rows, cols), F32),
            pltpu.VMEM((NA, cells), BF16),
            pltpu.VMEM((3 * NA, cells), BF16),
            pltpu.VMEM((3 * members, cells), BF16),
            pltpu.VMEM((cols, cols), F32),
            pltpu.VMEM((4, rows, cols), F32),
            pltpu.VMEM((4, rows, cols), jnp.int32),
            pltpu.VMEM((NU, 2, members, cols), F32),
            pltpu.VMEM((NU, 2, rows, cols), F32),
            pltpu.VMEM((NU, 2, members, cols), F32),
            pltpu.VMEM((NU, rows, cols), F32),
            pltpu.VMEM((NX0, members, cols), F32),
            pltpu.VMEM((NX0, 4, members, cols), F32),
            pltpu.VMEM((LEVELS + 1, NA, cols), F32),
            pltpu.VMEM((LEVELS, NA, cols), F32),
            pltpu.VMEM((LEVELS + 1, members, cols), F32),
            pltpu.VMEM((LEVELS, members, cols), F32),
            pltpu.VMEM((2, 5 * cols, cols), BF16),
            pltpu.VMEM((LEVELS - 1, 2, NA, cols), BF16),
            pltpu.VMEM((LEVELS, cols, cols), BF16),
            pltpu.SemaphoreType.DMA((slots,)),
            pltpu.SemaphoreType.DMA((slots,)),
        ],
        compiler_params=pltpu.CompilerParams(collective_id=0, has_side_effects=True),
    )(source, guess, conductivity, storage, aggregates, pair_maps.reshape(LEVELS, -1))


def solution(mesh):
    placed = (
        P(None, "row", "col"),
        P(None, "row", "col"),
        P("row", "col"),
        P("row", "col"),
        P("row", "col"),
        P(None, "row", "col", None),
    )
    return jax.shard_map(
        functools.partial(shards, mesh.shape["row"], mesh.shape["col"]),
        mesh=mesh,
        in_specs=placed,
        out_specs=(P(None, "row", "col"), P(None, "row", "col")),
        check_vma=False,
    )
```

```python
import functools

import jax
import jax.numpy as jnp
from jax import lax
from jax.experimental import pallas as pl
from jax.experimental.pallas import tpu as pltpu
from jax.sharding import PartitionSpec as P

NA = 64
SWEEPS = 3
LEVELS = 4
OMEGA_FINE = 0.8
OMEGA_COARSE = 0.6
F32 = jnp.float32
BF16 = jnp.bfloat16
MESH = pl.DeviceIdType.MESH
OPP = (1, 0, 3, 2, 7, 6, 5, 4)
WIDE = SWEEPS + 1
GROUP = 2 * WIDE
NX0 = 2 * SWEEPS
NN = (((1,), (0,)), ((), ()))
NT = (((1,), (1,)), ((), ()))


def dg(a, b, dims):
    return lax.dot_general(a, b, dims, preferred_element_type=F32)


def split2(x):
    hi = x.astype(BF16)
    return hi, (x - hi.astype(F32)).astype(BF16)


def split3(x):
    hi = x.astype(BF16)
    rest = x - hi.astype(F32)
    mid = rest.astype(BF16)
    return hi, mid, (rest - mid.astype(F32)).astype(BF16)


def dot_parts(x, w_hi, w_lo):
    hi, lo = split2(x)
    return dg(hi, w_hi, NN) + (dg(lo, w_hi, NN) + dg(hi, w_lo, NN))


def dot_hot(x, hot, dims):
    hi, mid, lo = split3(x)
    return dg(hi, hot, dims) + (dg(mid, hot, dims) + dg(lo, hot, dims))


def hot_dot(hot, x, dims):
    hi, mid, lo = split3(x)
    return dg(hot, hi, dims) + (dg(hot, mid, dims) + dg(hot, lo, dims))


def kernel(n_row, n_col, src, guess, cond, sto, agg, pm, sol, res,
           u, se, left, mo, gmat, rlhs, xt, crecv, srecv, ccorn, scorn, arecv, rowbuf, colbuf, corner,
           rsend, csend, xsend, xrecv, msend, mrecv, vsend, vrecv, wmat, bsp, qts, ssem, rsem):
    members, rows, cols = guess.shape
    ext = rows + GROUP
    row = lax.axis_index("row")
    col = lax.axis_index("col")
    has = [row > 0, row < n_row - 1, col > 0, col < n_col - 1]
    dev = [(row - 1, col), (row + 1, col), (row, col - 1), (row, col + 1)]
    for v in (0, 1):
        for h in (2, 3):
            has.append(jnp.logical_and(has[v], has[h]))
            dev.append((dev[v][0], dev[h][1]))
    col_bit = col % 2
    row_bit = row % 2
    col_bit2 = col // 2 % 2
    row_bit2 = row // 2 % 2
    upper = (col_bit, row_bit, col_bit2, row_bit2)
    partner = (
        (row, col + 1 - 2 * col_bit),
        (row + 1 - 2 * row_bit, col),
        (row, col + 2 - 4 * col_bit2),
        (row + 2 - 4 * row_bit2, col),
    )

    barrier = pltpu.get_barrier_semaphore()
    count = jnp.int32(2)
    for d in range(8):
        count = count + has[d].astype(jnp.int32)

        @pl.when(has[d])
        def _():
            pl.semaphore_signal(barrier, inc=1, device_id=dev[d], device_id_type=MESH)

    for k in (2, 3):
        pl.semaphore_signal(barrier, inc=1, device_id=partner[k], device_id_type=MESH)

    def copy(source, target, slot, device):
        return pltpu.make_async_remote_copy(
            src_ref=source, dst_ref=target, send_sem=ssem.at[slot], recv_sem=rsem.at[slot],
            device_id=device, device_id_type=MESH)

    sent = []

    def start(d, source, target, slot):
        @pl.when(has[d])
        def _():
            copy(source, target, slot, dev[d]).start()

        sent.append((d, source, target, slot))

    def arrive(d, source, target, slot):
        @pl.when(has[OPP[d]])
        def _():
            copy(source, target, slot, dev[d]).wait_recv()

    for d in range(8):
        @pl.when(jnp.logical_not(has[OPP[d]]))
        def _():
            for got, got_corner in ((crecv, ccorn), (srecv, scorn)):
                if d < 4:
                    got[d] = jnp.ones((rows, cols), F32)
                else:
                    got_corner[d - 4] = jnp.ones((GROUP, cols), F32)
            if d < 4:
                arecv[d] = jnp.zeros((rows, cols), jnp.int32)
                for e in range(NX0):
                    xrecv[e, d] = jnp.zeros((members, cols), F32)
            for p in range(3):
                if d < 2:
                    rowbuf[p, d] = jnp.zeros((WIDE * members, cols), F32)
                elif d < 4:
                    colbuf[p, d - 2] = jnp.zeros((rows, cols), F32)
                else:
                    corner[p, d - 4] = jnp.zeros((GROUP, cols), F32)

    lane = lax.broadcasted_iota(jnp.int32, (ext, cols), 1)
    sub = lax.broadcasted_iota(jnp.int32, (ext, cols), 0)
    l8 = lane % GROUP
    owner = lane // GROUP
    lane8 = lane[0:GROUP]
    sub8 = sub[0:GROUP]

    def mirror(x):
        where = lax.broadcasted_iota(jnp.int32, x.shape, 1)
        bit = 1
        while bit < GROUP:
            x = jnp.where(where // bit % 2 == 0, pltpu.roll(x, cols - bit, 1), pltpu.roll(x, bit, 1))
            bit *= 2
        return x

    def repeat(x):
        width = GROUP
        while width < cols:
            x = x + pltpu.roll(x, width, 1)
            width *= 2
        return x

    def halo_ref(p, d):
        source = rsend.at[p, d] if d < 2 else csend.at[p] if d < 4 else csend.at[
            p, pl.ds(0 if d < 6 else rows - GROUP, GROUP)]
        target = rowbuf.at[p, d] if d < 2 else colbuf.at[p, d - 2] if d < 4 else corner.at[p, d - 4]
        return d, source, target, 20 + 8 * p + d

    def part_ref(value, plane, corners, d, slot):
        if d in (2, 3):
            return d, value, plane.at[d], slot
        source = value.at[pl.ds(0 if d in (0, 4, 5) else rows - GROUP, GROUP)]
        target = plane.at[d, pl.ds(0, GROUP)] if d < 2 else corners.at[d - 4]
        return d, source, target, slot

    def pack(p, field_of):
        packed = jnp.zeros((rows, cols), F32)
        for m in range(members):
            v = field_of(m)
            packed = jnp.where(owner[0:rows] == m, pltpu.roll(v, (GROUP * m + WIDE) % cols, 1), packed)
            rsend[p, 0, WIDE * m : WIDE * (m + 1), :] = v[0:WIDE]
            rsend[p, 1, WIDE * m : WIDE * (m + 1), :] = v[rows - WIDE : rows]
        csend[p] = mirror(packed)

    order = (2, 3, 4, 5, 6, 7, 0, 1)

    def halo_start(p):
        for d in order:
            start(*halo_ref(p, d))

    def halo_arrive(p):
        for d in range(8):
            arrive(*halo_ref(p, d))

    def under(south, north):
        return jnp.where(sub8 < WIDE, south, north)

    def halo_fill(p, field):
        for m in range(members):
            field[m, rows : rows + WIDE, :] = rowbuf[p, 0, WIDE * m : WIDE * (m + 1), :]
            field[m, rows + WIDE : ext, :] = rowbuf[p, 1, WIDE * m : WIDE * (m + 1), :]
        side_e = jnp.concatenate([colbuf[p, 0], under(corner[p, 0], corner[p, 2])], axis=0)
        side_w = jnp.concatenate([colbuf[p, 1], under(corner[p, 1], corner[p, 3])], axis=0)
        return jnp.where(l8 < WIDE, side_e, side_w)

    def cond_parts(d):
        return part_ref(cond, crecv, ccorn, d, d)

    def sto_parts(d):
        return part_ref(sto, srecv, scorn, d, 8 + d)

    pack(0, lambda m: guess[m])
    pl.semaphore_wait(barrier, count)
    for d in order:
        start(*cond_parts(d))
        start(*sto_parts(d))
    halo_start(0)
    for d in range(4):
        start(d, agg, arecv.at[d], 16 + d)
    pack(1, lambda m: src[m])
    halo_start(1)

    agg_v = agg[...]
    sub64 = lax.broadcasted_iota(jnp.int32, (NA, cols), 0)
    for r in range(rows):
        mo[:, r * cols : (r + 1) * cols] = jnp.where(
            sub64 == agg_v[r : r + 1], 1.0, 0.0).astype(BF16)
    wmat[...] = jnp.zeros(wmat.shape, BF16)
    msend[...] = jnp.zeros(msend.shape, F32)
    xt[...] = jnp.zeros(xt.shape, F32)
    iota128 = lax.broadcasted_iota(jnp.int32, (cols, cols), 0)
    for k in range(LEVELS):
        pmk = pm[k : k + 1, :]
        pmk = jnp.where(upper[k] == 1, pltpu.roll(pmk, NA, 1), pmk)
        qts[k] = jnp.where(iota128 == pmk, 1.0, 0.0).astype(BF16)

    for d in range(8):
        arrive(*cond_parts(d))
        arrive(*sto_parts(d))

    def extend(value, plane, corners):
        main = jnp.concatenate([value[...], under(plane[0, 0:GROUP], plane[1, 0:GROUP])], axis=0)
        side_e = jnp.concatenate([plane[2], under(corners[0], corners[2])], axis=0)
        side_w = jnp.concatenate([plane[3], under(corners[1], corners[3])], axis=0)
        base = jnp.where(lane < WIDE, pltpu.roll(side_w, WIDE, 1), pltpu.roll(side_e, WIDE, 1))
        side = mirror(repeat(jnp.where(lane < GROUP, base, 0.0)))
        return main, side

    cm, cs = extend(cond, crecv, ccorn)
    sm, ss = extend(sto, srecv, scorn)
    last = rows - 1
    hasi = [h.astype(jnp.int32) for h in has[0:4]]

    def face(a, b):
        return 2.0 * (a * b) / (a + b)

    def vertical(x):
        down = jnp.where(jnp.logical_and(sub == last, hasi[1] == 0), 0.0, face(x, pltpu.roll(x, ext - 1, 0)))
        up = jnp.where(jnp.logical_and(sub == 0, hasi[0] == 0), 0.0, face(x, pltpu.roll(x, 1, 0)))
        return down, up

    side_at = pltpu.roll(cs, cols - WIDE, 1)
    rim = jnp.logical_and(lane >= WIDE - 1, lane <= WIDE)
    main_at = repeat(jnp.where(rim, pltpu.roll(cm, WIDE, 1), 0.0))
    east = face(cm, jnp.where(lane == cols - 1, side_at, pltpu.roll(cm, cols - 1, 1)))
    west = face(cm, jnp.where(lane == 0, side_at, pltpu.roll(cm, 1, 1)))
    east = jnp.where(lane < cols - 1 + hasi[3], east, 0.0)
    west = jnp.where(lane >= 1 - hasi[2], west, 0.0)
    south, north = vertical(cm)
    diag = sm + east + west + south + north
    step = OMEGA_FINE / diag
    s_west = face(cs, jnp.where(l8 == WIDE - 1, main_at, pltpu.roll(cs, cols - 1, 1)))
    s_east = face(cs, jnp.where(l8 == WIDE, main_at, pltpu.roll(cs, 1, 1)))
    s_west = jnp.where(jnp.logical_and(l8 == WIDE - 1, hasi[3] == 0), 0.0, s_west)
    s_east = jnp.where(jnp.logical_and(l8 == WIDE, hasi[2] == 0), 0.0, s_east)
    s_south, s_north = vertical(cs)
    s_diag = ss + s_east + s_west + s_south + s_north
    s_step = OMEGA_FINE / s_diag

    def apply_field(side, n, finish):
        lane_n = lane[0:n]
        edge = jnp.zeros((ext, cols), F32)
        for m in range(members):
            v = u[m]
            hm = pltpu.roll(side, (2 * cols - GROUP * m - WIDE) % cols, 1)[0:n]
            vn = v[0:n]
            from_w = jnp.where(lane_n == 0, hm, pltpu.roll(vn, 1, 1))
            from_e = jnp.where(lane_n == cols - 1, hm, pltpu.roll(vn, cols - 1, 1))
            from_s = pltpu.roll(v, ext - 1, 0)[0:n]
            from_n = pltpu.roll(v, 1, 0)[0:n]
            rest = se[m, 0:n] - (diag[0:n] * vn - (
                east[0:n] * from_e + west[0:n] * from_w + south[0:n] * from_s + north[0:n] * from_n))
            if n == ext:
                edge = jnp.where(owner == m, pltpu.roll(v, (GROUP * m + WIDE) % cols, 1), edge)
            finish(m, vn, rest)
        return edge

    def sweep(side, s_src):
        def finish(m, v, rest):
            u[m] = v + step * rest

        edge = apply_field(side, ext, finish)
        from_w = jnp.where(l8 == WIDE - 1, edge, pltpu.roll(side, cols - 1, 1))
        from_e = jnp.where(l8 == WIDE, edge, pltpu.roll(side, 1, 1))
        rest = s_src - (s_diag * side - (s_east * from_e + s_west * from_w
                        + s_south * pltpu.roll(side, ext - 1, 0) + s_north * pltpu.roll(side, 1, 0)))
        return side + s_step * rest

    in_east = jnp.where(lane < cols - 1, east, 0.0)
    in_south = jnp.where(sub < last, south, 0.0)
    right = pltpu.roll(agg_v, cols - 1, 1)
    below = pltpu.roll(agg_v, last, 0)
    half = 0.5 * diag
    for r in range(rows):
        s = slice(r, r + 1)
        g = (jnp.where(sub64 == right[s], in_east[s], 0.0)
             + jnp.where(sub64 == below[s], in_south[s], 0.0)
             - jnp.where(sub64 == agg_v[s], half[s], 0.0))
        for i, part in enumerate(split3(g)):
            gmat[i * NA : (i + 1) * NA, r * cols : (r + 1) * cols] = part
    gx = dg(gmat[...], mo[...], NT)
    xt[0:NA, 0:NA] = gx[0:NA] + (gx[NA : 2 * NA] + gx[2 * NA : 3 * NA])
    xfull = xt[...]
    block = -(xfull + xfull.T)[0:NA]
    msend[0] = block

    def mat_copy(k):
        return copy(msend.at[k], mrecv.at[k], 44 + 4 * NX0 + k, partner[k])

    def vec_copy(k):
        return copy(vsend.at[k], vrecv.at[k], 44 + 4 * NX0 + LEVELS + k, partner[k])

    mat_copy(0).start()

    lane_c = lax.broadcasted_iota(jnp.int32, (NA, cols), 1)
    lane_1 = lax.broadcasted_iota(jnp.int32, (1, cols), 1)

    def weight(mat):
        d = jnp.sum(jnp.where(lane_c == sub64, mat, 0.0), axis=0, keepdims=True)
        ok = lane_1 < NA
        return jnp.where(ok, OMEGA_COARSE / jnp.where(ok, d, 1.0), 0.0)

    weights = [weight(block)]

    def next_mat(k):
        mat_copy(k).wait_recv()
        both = jnp.concatenate([msend[k], pltpu.roll(mrecv[k], NA, 1)], axis=0)
        qt = qts[k]
        mat = hot_dot(qt[0:NA], dot_hot(both, qt, NT), NN)
        msend[k + 1] = mat
        if k + 1 < LEVELS:
            mat_copy(k + 1).start()
            hi, lo = split2(mat)
            bsp[k, 0] = hi
            bsp[k, 1] = lo
            weights.append(weight(mat))

    for d in range(4):
        arrive(d, agg, arecv.at[d], 16 + d)
    agg_t = agg_v.astype(F32).T.astype(jnp.int32)

    def couple(slot, own_ids, other_ids, faces, width):
        own = jnp.where(lax.broadcasted_iota(jnp.int32, (cols, width), 0) == own_ids, 1.0, 0.0).astype(BF16)
        other = jnp.where(lax.broadcasted_iota(jnp.int32, (NA, width), 0) == other_ids, faces, 0.0)
        hi, lo = split2(-dot_hot(other, own, NT))
        wmat[0, slot * cols : slot * cols + NA] = hi
        wmat[1, slot * cols : slot * cols + NA] = lo

    hi, lo = split2(block)
    wmat[0, 0:NA] = hi
    wmat[1, 0:NA] = lo
    couple(1, agg_v[last:rows], arecv[0][0:1], south[last:rows], cols)
    couple(2, agg_v[0:1], arecv[1][last : rows], north[0:1], cols)
    agg_e = arecv[2].astype(F32).T.astype(jnp.int32)
    agg_w = arecv[3].astype(F32).T.astype(jnp.int32)
    couple(3, agg_t[cols - 1 : cols], agg_e[0:1], east[0:rows].T[cols - 1 : cols], rows)
    couple(4, agg_t[0:1], agg_w[cols - 1 : cols], west[0:rows].T[0:1], rows)
    for m in range(members):
        u[m, 0:rows] = guess[m]
        se[m, 0:rows] = src[m]
    halo_arrive(0)
    side = halo_fill(0, u)
    halo_arrive(1)
    s_src = halo_fill(1, se)
    for _ in range(SWEEPS):
        side = sweep(side, s_src)

    def keep_left(m, v, rest):
        left[m] = rest

    apply_field(side, rows, keep_left)
    for r in range(rows):
        for i, part in enumerate(split3(left[:, r, :])):
            rlhs[i * members : (i + 1) * members, r * cols : (r + 1) * cols] = part
    gr = dg(rlhs[...], mo[...], NT)
    vsend[LEVELS] = jnp.zeros((members, cols), F32)
    vsend[LEVELS, :, 0:NA] = gr[0:members] + (gr[members : 2 * members] + gr[2 * members : 3 * members])
    y0 = vsend[LEVELS]

    def x_slot(e, d):
        return (d, xsend.at[e], xrecv.at[e, d], 44 + 4 * e + d)

    def level_one(e, x, between=None):
        xsend[e] = x
        for d in (2, 3, 0, 1):
            start(*x_slot(e, d))
        if between is not None:
            between()
        for d in range(4):
            arrive(*x_slot(e, d))
        every = jnp.concatenate([x] + [xrecv[e, d] for d in range(4)], axis=1)
        return dot_parts(every, wmat[0], wmat[1])

    inverse = []

    def last_mat():
        next_mat(3)
        mat = jnp.where(lane_c < NA, msend[LEVELS], jnp.where(lane_c - NA == sub64, 1.0, 0.0))
        for k in range(NA):
            pivot = mat[k : k + 1] / mat[k : k + 1, k : k + 1]
            mat = jnp.where(sub64 == k, pivot, mat - mat[:, k : k + 1] * pivot)
        inverse.append(jnp.where(lane_c < NA, pltpu.roll(mat, NA, 1), 0.0))

    x = y0 * weights[0]
    x = x + (y0 - level_one(0, x, lambda: next_mat(0))) * weights[0]
    x = x + (y0 - level_one(1, x, lambda: next_mat(1))) * weights[0]
    rem = y0 - level_one(2, x, lambda: next_mat(2))
    sols, rhss = [x], [y0]
    for k in range(LEVELS):
        vsend[k] = rem
        vec_copy(k).start()
        if k == 1:
            last_mat()
        vec_copy(k).wait_recv()
        y = dot_hot(rem + pltpu.roll(vrecv[k], NA, 1), qts[k], NT)
        rhss.append(y)
        if k < LEVELS - 1:
            apply_c = lambda z: dot_parts(z[:, 0:NA], bsp[k, 0], bsp[k, 1])
            w = weights[k + 1]
            x = y * w
            for _ in range(SWEEPS - 1):
                x = x + (y - apply_c(x)) * w
            rem = y - apply_c(x)
        else:
            x = lax.dot_general(y[:, 0:NA], inverse[0], NN, precision=lax.Precision.HIGHEST,
                                preferred_element_type=F32)
        sols.append(x)
    lane_m = lax.broadcasted_iota(jnp.int32, (members, cols), 1)
    for k in reversed(range(LEVELS)):
        x = sols[k] + jnp.where(lane_m < NA, dot_hot(x, qts[k], NN), 0.0)
        for i in range(SWEEPS):
            if k > 0:
                applied = dot_parts(x[:, 0:NA], bsp[k - 1, 0], bsp[k - 1, 1])
            else:
                applied = level_one(SWEEPS + i, x)
            x = x + (rhss[k] - applied) * weights[k]

    for r in range(rows):
        part = dot_hot(x[:, 0:NA], mo[:, r * cols : (r + 1) * cols], NN)
        u[:, r, :] = u[:, r, :] + part
    pack(2, lambda m: u[m, 0:rows])
    halo_start(2)
    halo_arrive(2)
    side = halo_fill(2, u)
    for _ in range(SWEEPS):
        side = sweep(side, s_src)

    def out(m, v, rest):
        sol[m] = v
        res[m] = rest

    apply_field(side, rows, out)
    for d, source, target, slot in sent:
        @pl.when(has[d])
        def _():
            copy(source, target, slot, dev[d]).wait_send()

    for k in range(LEVELS):
        mat_copy(k).wait_send()
        vec_copy(k).wait_send()


def shards(n_row, n_col, source, guess, conductivity, storage, aggregates, pair_maps):
    members, rows, cols = source.shape
    cells = rows * cols
    ext = rows + GROUP
    vm = pl.BlockSpec(memory_space=pltpu.VMEM)
    slots = 44 + 4 * NX0 + 2 * LEVELS
    return pl.pallas_call(
        functools.partial(kernel, n_row, n_col),
        out_shape=(jax.ShapeDtypeStruct(source.shape, F32),) * 2,
        in_specs=[vm] * 6,
        out_specs=(vm, vm),
        scratch_shapes=[
            pltpu.VMEM((members, ext, cols), F32),
            pltpu.VMEM((members, ext, cols), F32),
            pltpu.VMEM((members, rows, cols), F32),
            pltpu.VMEM((NA, cells), BF16),
            pltpu.VMEM((3 * NA, cells), BF16),
            pltpu.VMEM((3 * members, cells), BF16),
            pltpu.VMEM((cols, cols), F32),
            pltpu.VMEM((4, rows, cols), F32),
            pltpu.VMEM((4, rows, cols), F32),
            pltpu.VMEM((4, GROUP, cols), F32),
            pltpu.VMEM((4, GROUP, cols), F32),
            pltpu.VMEM((4, rows, cols), jnp.int32),
            pltpu.VMEM((3, 2, WIDE * members, cols), F32),
            pltpu.VMEM((3, 2, rows, cols), F32),
            pltpu.VMEM((3, 4, GROUP, cols), F32),
            pltpu.VMEM((3, 2, WIDE * members, cols), F32),
            pltpu.VMEM((3, rows, cols), F32),
            pltpu.VMEM((NX0, members, cols), F32),
            pltpu.VMEM((NX0, 4, members, cols), F32),
            pltpu.VMEM((LEVELS + 1, NA, cols), F32),
            pltpu.VMEM((LEVELS, NA, cols), F32),
            pltpu.VMEM((LEVELS + 1, members, cols), F32),
            pltpu.VMEM((LEVELS, members, cols), F32),
            pltpu.VMEM((2, 5 * cols, cols), BF16),
            pltpu.VMEM((LEVELS - 1, 2, NA, cols), BF16),
            pltpu.VMEM((LEVELS, cols, cols), BF16),
            pltpu.SemaphoreType.DMA((slots,)),
            pltpu.SemaphoreType.DMA((slots,)),
        ],
        compiler_params=pltpu.CompilerParams(collective_id=0, has_side_effects=True),
    )(source, guess, conductivity, storage, aggregates, pair_maps.reshape(LEVELS, -1))


def solution(mesh):
    placed = (
        P(None, "row", "col"),
        P(None, "row", "col"),
        P("row", "col"),
        P("row", "col"),
        P("row", "col"),
        P(None, "row", "col", None),
    )
    return jax.shard_map(
        functools.partial(shards, mesh.shape["row"], mesh.shape["col"]),
        mesh=mesh,
        in_specs=placed,
        out_specs=(P(None, "row", "col"), P(None, "row", "col")),
        check_vma=False,
    )
```

```python
import functools

import jax
import jax.numpy as jnp
from jax import lax
from jax.experimental import pallas as pl
from jax.experimental.pallas import tpu as pltpu
from jax.sharding import PartitionSpec as P

NA = 64
SWEEPS = 3
LEVELS = 4
OMEGA_FINE = 0.8
OMEGA_COARSE = 0.6
F32 = jnp.float32
BF16 = jnp.bfloat16
MESH = pl.DeviceIdType.MESH
OPP = (1, 0, 3, 2, 7, 6, 5, 4)
WIDE = SWEEPS + 1
GROUP = 2 * WIDE
NX0 = 2 * SWEEPS
NN = (((1,), (0,)), ((), ()))
NT = (((1,), (1,)), ((), ()))


def dg(a, b, dims):
    return lax.dot_general(a, b, dims, preferred_element_type=F32)


def split2(x):
    hi = x.astype(BF16)
    return hi, (x - hi.astype(F32)).astype(BF16)


def split3(x):
    hi = x.astype(BF16)
    rest = x - hi.astype(F32)
    mid = rest.astype(BF16)
    return hi, mid, (rest - mid.astype(F32)).astype(BF16)


def dot_parts(x, w_hi, w_lo, dims=NN):
    hi, lo = split2(x)
    return dg(hi, w_hi, dims) + (dg(lo, w_hi, dims) + dg(hi, w_lo, dims))


def dot_hot(x, hot, dims):
    hi, mid, lo = split3(x)
    return dg(hi, hot, dims) + (dg(mid, hot, dims) + dg(lo, hot, dims))


def hot_dot(hot, x, dims):
    hi, mid, lo = split3(x)
    return dg(hot, hi, dims) + (dg(hot, mid, dims) + dg(hot, lo, dims))


def kernel(n_row, n_col, src, guess, cond, sto, agg, pm, sol, res,
           u, se, left, mo, gmat, rlhs, xt, crecv, srecv, ccorn, scorn, arecv, rowbuf, colbuf, corner,
           rsend, csend, xsend, xrecv, msend, mrecv, vsend, vrecv, wmat, bsp, qts, ssem, rsem):
    members, rows, cols = guess.shape
    ext = rows + GROUP
    row = lax.axis_index("row")
    col = lax.axis_index("col")
    has = [row > 0, row < n_row - 1, col > 0, col < n_col - 1]
    dev = [(row - 1, col), (row + 1, col), (row, col - 1), (row, col + 1)]
    for v in (0, 1):
        for h in (2, 3):
            has.append(jnp.logical_and(has[v], has[h]))
            dev.append((dev[v][0], dev[h][1]))
    col_bit = col % 2
    row_bit = row % 2
    col_bit2 = col // 2 % 2
    row_bit2 = row // 2 % 2
    upper = (col_bit, row_bit, col_bit2, row_bit2)
    partner = (
        (row, col + 1 - 2 * col_bit),
        (row + 1 - 2 * row_bit, col),
        (row, col + 2 - 4 * col_bit2),
        (row + 2 - 4 * row_bit2, col),
    )

    barrier = pltpu.get_barrier_semaphore()
    count = jnp.int32(2)
    for d in range(8):
        count = count + has[d].astype(jnp.int32)

        @pl.when(has[d])
        def _():
            pl.semaphore_signal(barrier, inc=1, device_id=dev[d], device_id_type=MESH)

    for k in (2, 3):
        pl.semaphore_signal(barrier, inc=1, device_id=partner[k], device_id_type=MESH)

    def copy(source, target, slot, device):
        return pltpu.make_async_remote_copy(
            src_ref=source, dst_ref=target, send_sem=ssem.at[slot], recv_sem=rsem.at[slot],
            device_id=device, device_id_type=MESH)

    sent = []

    def start(d, source, target, slot):
        @pl.when(has[d])
        def _():
            copy(source, target, slot, dev[d]).start()

        sent.append((d, source, target, slot))

    def arrive(d, source, target, slot):
        @pl.when(has[OPP[d]])
        def _():
            copy(source, target, slot, dev[d]).wait_recv()

    for d in range(8):
        @pl.when(jnp.logical_not(has[OPP[d]]))
        def _():
            for got, got_corner in ((crecv, ccorn), (srecv, scorn)):
                if d < 4:
                    got[d] = jnp.ones((rows, cols), F32)
                else:
                    got_corner[d - 4] = jnp.ones((GROUP, cols), F32)
            if d < 4:
                arecv[d] = jnp.zeros((rows, cols), jnp.int32)
                for e in range(NX0):
                    xrecv[e, d] = jnp.zeros((members, cols), F32)
            for p in range(3):
                if d < 2:
                    rowbuf[p, d] = jnp.zeros((WIDE * members, cols), F32)
                elif d < 4:
                    colbuf[p, d - 2] = jnp.zeros((rows, cols), F32)
                else:
                    corner[p, d - 4] = jnp.zeros((GROUP, cols), F32)

    lane = lax.broadcasted_iota(jnp.int32, (ext, cols), 1)
    sub = lax.broadcasted_iota(jnp.int32, (ext, cols), 0)
    l8 = lane % GROUP
    owner = lane // GROUP
    lane8 = lane[0:GROUP]
    sub8 = sub[0:GROUP]

    def mirror(x):
        where = lax.broadcasted_iota(jnp.int32, x.shape, 1)
        bit = 1
        while bit < GROUP:
            x = jnp.where(where // bit % 2 == 0, pltpu.roll(x, cols - bit, 1), pltpu.roll(x, bit, 1))
            bit *= 2
        return x

    def repeat(x):
        width = GROUP
        while width < cols:
            x = x + pltpu.roll(x, width, 1)
            width *= 2
        return x

    def halo_ref(p, d):
        source = rsend.at[p, d] if d < 2 else csend.at[p] if d < 4 else csend.at[
            p, pl.ds(0 if d < 6 else rows - GROUP, GROUP)]
        target = rowbuf.at[p, d] if d < 2 else colbuf.at[p, d - 2] if d < 4 else corner.at[p, d - 4]
        return d, source, target, 20 + 8 * p + d

    def part_ref(value, plane, corners, d, slot):
        if d in (2, 3):
            return d, value, plane.at[d], slot
        source = value.at[pl.ds(0 if d in (0, 4, 5) else rows - GROUP, GROUP)]
        target = plane.at[d, pl.ds(0, GROUP)] if d < 2 else corners.at[d - 4]
        return d, source, target, slot

    def pack(p, field_of):
        packed = jnp.zeros((rows, cols), F32)
        for m in range(members):
            v = field_of(m)
            packed = jnp.where(owner[0:rows] == m, pltpu.roll(v, (GROUP * m + WIDE) % cols, 1), packed)
            rsend[p, 0, WIDE * m : WIDE * (m + 1), :] = v[0:WIDE]
            rsend[p, 1, WIDE * m : WIDE * (m + 1), :] = v[rows - WIDE : rows]
        csend[p] = mirror(packed)

    order = (2, 3, 4, 5, 6, 7, 0, 1)

    def halo_start(p):
        for d in order:
            start(*halo_ref(p, d))

    def halo_arrive(p):
        for d in range(8):
            arrive(*halo_ref(p, d))

    def under(south, north):
        return jnp.where(sub8 < WIDE, south, north)

    def halo_fill(p, field):
        for m in range(members):
            field[m, rows : rows + WIDE, :] = rowbuf[p, 0, WIDE * m : WIDE * (m + 1), :]
            field[m, rows + WIDE : ext, :] = rowbuf[p, 1, WIDE * m : WIDE * (m + 1), :]
        side_e = jnp.concatenate([colbuf[p, 0], under(corner[p, 0], corner[p, 2])], axis=0)
        side_w = jnp.concatenate([colbuf[p, 1], under(corner[p, 1], corner[p, 3])], axis=0)
        return jnp.where(l8 < WIDE, side_e, side_w)

    def cond_parts(d):
        return part_ref(cond, crecv, ccorn, d, d)

    def sto_parts(d):
        return part_ref(sto, srecv, scorn, d, 8 + d)

    pack(0, lambda m: guess[m])
    pack(1, lambda m: src[m])
    pl.semaphore_wait(barrier, count)
    for d in order:
        start(*cond_parts(d))
    for d in range(4):
        start(d, agg, arecv.at[d], 16 + d)
    for d in order:
        start(*sto_parts(d))
    halo_start(0)
    halo_start(1)

    agg_v = agg[...]
    sub64 = lax.broadcasted_iota(jnp.int32, (NA, cols), 0)
    for r in range(rows):
        mo[:, r * cols : (r + 1) * cols] = jnp.where(
            sub64 == agg_v[r : r + 1], 1.0, 0.0).astype(BF16)
    wmat[...] = jnp.zeros(wmat.shape, BF16)
    msend[...] = jnp.zeros(msend.shape, F32)
    xt[...] = jnp.zeros(xt.shape, F32)
    iota128 = lax.broadcasted_iota(jnp.int32, (cols, cols), 0)
    for k in range(LEVELS):
        pmk = pm[k : k + 1, :]
        pmk = jnp.where(upper[k] == 1, pltpu.roll(pmk, NA, 1), pmk)
        qts[k] = jnp.where(iota128 == pmk, 1.0, 0.0).astype(BF16)

    def face(a, b):
        return 2.0 * (a * b) / (a + b)

    last = rows - 1
    c = cond[...]
    in_east = jnp.where(lane[0:rows] < cols - 1, face(c, pltpu.roll(c, cols - 1, 1)), 0.0)
    in_south = jnp.where(sub[0:rows] < last, face(c, pltpu.roll(c, last, 0)), 0.0)
    right = pltpu.roll(agg_v, cols - 1, 1)
    below = pltpu.roll(agg_v, last, 0)
    half = 0.5 * (sto[...] + in_east + pltpu.roll(in_east, 1, 1) + in_south + pltpu.roll(in_south, 1, 0))
    for r in range(rows):
        s = slice(r, r + 1)
        g = (jnp.where(sub64 == right[s], in_east[s], 0.0)
             + jnp.where(sub64 == below[s], in_south[s], 0.0)
             - jnp.where(sub64 == agg_v[s], half[s], 0.0))
        for i, part in enumerate(split3(g)):
            gmat[i * NA : (i + 1) * NA, r * cols : (r + 1) * cols] = part
    gx = dg(gmat[...], mo[...], NT)
    xt[0:NA, 0:NA] = gx[0:NA] + (gx[NA : 2 * NA] + gx[2 * NA : 3 * NA])
    xfull = xt[...]
    inner = -(xfull + xfull.T)[0:NA]

    for d in range(8):
        arrive(*cond_parts(d))
        arrive(*sto_parts(d))

    def extend(value, plane, corners):
        main = jnp.concatenate([value[...], under(plane[0, 0:GROUP], plane[1, 0:GROUP])], axis=0)
        side_e = jnp.concatenate([plane[2], under(corners[0], corners[2])], axis=0)
        side_w = jnp.concatenate([plane[3], under(corners[1], corners[3])], axis=0)
        base = jnp.where(lane < WIDE, pltpu.roll(side_w, WIDE, 1), pltpu.roll(side_e, WIDE, 1))
        side = mirror(repeat(jnp.where(lane < GROUP, base, 0.0)))
        return main, side

    cm, cs = extend(cond, crecv, ccorn)
    sm, ss = extend(sto, srecv, scorn)
    hasi = [h.astype(jnp.int32) for h in has[0:4]]

    def vertical(x):
        down = jnp.where(jnp.logical_and(sub == last, hasi[1] == 0), 0.0, face(x, pltpu.roll(x, ext - 1, 0)))
        up = jnp.where(jnp.logical_and(sub == 0, hasi[0] == 0), 0.0, face(x, pltpu.roll(x, 1, 0)))
        return down, up

    side_at = pltpu.roll(cs, cols - WIDE, 1)
    rim = jnp.logical_and(lane >= WIDE - 1, lane <= WIDE)
    main_at = repeat(jnp.where(rim, pltpu.roll(cm, WIDE, 1), 0.0))
    east = face(cm, jnp.where(lane == cols - 1, side_at, pltpu.roll(cm, cols - 1, 1)))
    west = face(cm, jnp.where(lane == 0, side_at, pltpu.roll(cm, 1, 1)))
    east = jnp.where(lane < cols - 1 + hasi[3], east, 0.0)
    west = jnp.where(lane >= 1 - hasi[2], west, 0.0)
    south, north = vertical(cm)
    diag = sm + east + west + south + north
    step = OMEGA_FINE / diag
    s_west = face(cs, jnp.where(l8 == WIDE - 1, main_at, pltpu.roll(cs, cols - 1, 1)))
    s_east = face(cs, jnp.where(l8 == WIDE, main_at, pltpu.roll(cs, 1, 1)))
    s_west = jnp.where(jnp.logical_and(l8 == WIDE - 1, hasi[3] == 0), 0.0, s_west)
    s_east = jnp.where(jnp.logical_and(l8 == WIDE, hasi[2] == 0), 0.0, s_east)
    s_south, s_north = vertical(cs)
    s_diag = ss + s_east + s_west + s_south + s_north
    s_step = OMEGA_FINE / s_diag

    def apply_field(side, n, finish):
        lane_n = lane[0:n]
        edge = jnp.zeros((ext, cols), F32)
        for m in range(members):
            v = u[m]
            hm = pltpu.roll(side, (2 * cols - GROUP * m - WIDE) % cols, 1)[0:n]
            vn = v[0:n]
            from_w = jnp.where(lane_n == 0, hm, pltpu.roll(vn, 1, 1))
            from_e = jnp.where(lane_n == cols - 1, hm, pltpu.roll(vn, cols - 1, 1))
            from_s = pltpu.roll(v, ext - 1, 0)[0:n]
            from_n = pltpu.roll(v, 1, 0)[0:n]
            rest = se[m, 0:n] - (diag[0:n] * vn - (
                east[0:n] * from_e + west[0:n] * from_w + south[0:n] * from_s + north[0:n] * from_n))
            if n == ext:
                edge = jnp.where(owner == m, pltpu.roll(v, (GROUP * m + WIDE) % cols, 1), edge)
            finish(m, vn, rest)
        return edge

    def sweep(side, s_src):
        def finish(m, v, rest):
            u[m] = v + step * rest

        edge = apply_field(side, ext, finish)
        from_w = jnp.where(l8 == WIDE - 1, edge, pltpu.roll(side, cols - 1, 1))
        from_e = jnp.where(l8 == WIDE, edge, pltpu.roll(side, 1, 1))
        rest = s_src - (s_diag * side - (s_east * from_e + s_west * from_w
                        + s_south * pltpu.roll(side, ext - 1, 0) + s_north * pltpu.roll(side, 1, 0)))
        return side + s_step * rest


    for d in range(4):
        arrive(d, agg, arecv.at[d], 16 + d)
    agg_t = agg_v.astype(F32).T.astype(jnp.int32)

    def couple(slot, own_ids, other_ids, faces, width):
        own = jnp.where(lax.broadcasted_iota(jnp.int32, (cols, width), 0) == own_ids, 1.0, 0.0).astype(BF16)
        other = jnp.where(lax.broadcasted_iota(jnp.int32, (NA, width), 0) == other_ids, faces, 0.0)
        links = dot_hot(other, own, NT)
        hi, lo = split2(-links)
        wmat[0, slot * cols : slot * cols + NA] = hi
        wmat[1, slot * cols : slot * cols + NA] = lo
        return jnp.sum(links, axis=0, keepdims=True)

    outer = couple(1, agg_v[last:rows], arecv[0][0:1], south[last:rows], cols)
    outer = outer + couple(2, agg_v[0:1], arecv[1][last : rows], north[0:1], cols)
    agg_e = arecv[2].astype(F32).T.astype(jnp.int32)
    agg_w = arecv[3].astype(F32).T.astype(jnp.int32)
    outer = outer + couple(3, agg_t[cols - 1 : cols], agg_e[0:1], east[0:rows].T[cols - 1 : cols], rows)
    outer = outer + couple(4, agg_t[0:1], agg_w[cols - 1 : cols], west[0:rows].T[0:1], rows)
    def mat_copy(k):
        return copy(msend.at[k], mrecv.at[k], 44 + 4 * NX0 + k, partner[k])

    def vec_copy(k):
        return copy(vsend.at[k], vrecv.at[k], 44 + 4 * NX0 + LEVELS + k, partner[k])

    lane_c = lax.broadcasted_iota(jnp.int32, (NA, cols), 1)
    lane_1 = lax.broadcasted_iota(jnp.int32, (1, cols), 1)

    def weight(mat):
        d = jnp.sum(jnp.where(lane_c == sub64, mat, 0.0), axis=0, keepdims=True)
        ok = lane_1 < NA
        return jnp.where(ok, OMEGA_COARSE / jnp.where(ok, d, 1.0), 0.0)

    def next_mat(k):
        mat_copy(k).wait_recv()
        both = jnp.concatenate([msend[k], pltpu.roll(mrecv[k], NA, 1)], axis=0)
        qt = qts[k]
        mat = hot_dot(qt[0:NA], dot_hot(both, qt, NT), NN)
        msend[k + 1] = mat
        if k + 1 < LEVELS:
            mat_copy(k + 1).start()
            eye = jnp.where(lane_c == sub64, 1.0, 0.0)
            side_w = OMEGA_COARSE / jnp.sum(eye * mat, axis=1, keepdims=True)
            one = eye - mat * weight(mat)
            hi, lo = split2(one)
            two = dot_parts(one[:, 0:NA], hi, lo)
            parts = split2(dot_parts(two[:, 0:NA], hi, lo)) + split2(side_w * (eye + one + two))
            for i in range(4):
                bsp[k, i, 0:NA] = parts[i]
                if i < 2:
                    bsp[k, i, NA:cols] = jnp.zeros((cols - NA, cols), BF16)

    block = inner + jnp.where(lane_c == sub64, outer, 0.0)
    msend[0] = block
    mat_copy(0).start()
    hi, lo = split2(block)
    wmat[0, 0:NA] = hi
    wmat[1, 0:NA] = lo
    weights = weight(block)

    for m in range(members):
        u[m, 0:rows] = guess[m]
        se[m, 0:rows] = src[m]
    halo_arrive(0)
    side = halo_fill(0, u)
    halo_arrive(1)
    s_src = halo_fill(1, se)
    for _ in range(SWEEPS):
        side = sweep(side, s_src)

    def keep_left(m, v, rest):
        left[m] = rest

    apply_field(side, rows, keep_left)
    for r in range(rows):
        for i, part in enumerate(split3(left[:, r, :])):
            rlhs[i * members : (i + 1) * members, r * cols : (r + 1) * cols] = part
    gr = dg(rlhs[...], mo[...], NT)
    vsend[LEVELS] = jnp.zeros((members, cols), F32)
    vsend[LEVELS, :, 0:NA] = gr[0:members] + (gr[members : 2 * members] + gr[2 * members : 3 * members])
    y0 = vsend[LEVELS]

    def x_slot(e, d):
        return (d, xsend.at[e], xrecv.at[e, d], 44 + 4 * e + d)

    def level_one(e, x, between=None):
        xsend[e] = x
        for d in (2, 3, 0, 1):
            start(*x_slot(e, d))
        if between is not None:
            between()
        for d in range(4):
            arrive(*x_slot(e, d))
        every = jnp.concatenate([x] + [xrecv[e, d] for d in range(4)], axis=1)
        return dot_parts(every, wmat[0], wmat[1])

    inverse = []

    def last_mat():
        next_mat(3)
        mat = jnp.where(lane_c < NA, msend[LEVELS], jnp.where(lane_c - NA == sub64, 1.0, 0.0))
        for k in range(NA):
            pivot = mat[k : k + 1] / mat[k : k + 1, k : k + 1]
            mat = jnp.where(sub64 == k, pivot, mat - mat[:, k : k + 1] * pivot)
        inverse.append(jnp.where(lane_c < NA, pltpu.roll(mat, NA, 1), 0.0))

    x = y0 * weights
    x = x + (y0 - level_one(0, x, lambda: next_mat(0))) * weights
    x = x + (y0 - level_one(1, x, lambda: next_mat(1))) * weights
    rem = y0 - level_one(2, x, lambda: next_mat(2))
    sols = [x]
    for k in range(LEVELS):
        vsend[k] = rem
        vec_copy(k).start()
        if k == 1:
            last_mat()
        vec_copy(k).wait_recv()
        y = dot_hot(rem + pltpu.roll(vrecv[k], NA, 1), qts[k], NT)
        if k < LEVELS - 1:
            rem = dot_parts(y, bsp[k, 0], bsp[k, 1], NT)
            x = dot_parts(y[:, 0:NA], bsp[k, 2, 0:NA], bsp[k, 3, 0:NA])
        else:
            x = lax.dot_general(y[:, 0:NA], inverse[0], NN, precision=lax.Precision.HIGHEST,
                                preferred_element_type=F32)
        sols.append(x)
    lane_m = lax.broadcasted_iota(jnp.int32, (members, cols), 1)
    for k in reversed(range(LEVELS)):
        x = sols[k] + jnp.where(lane_m < NA, dot_hot(x, qts[k], NN), 0.0)
        if k > 0:
            x = sols[k] + dot_parts(x[:, 0:NA], bsp[k - 1, 0, 0:NA], bsp[k - 1, 1, 0:NA])
        else:
            for i in range(SWEEPS):
                x = x + (y0 - level_one(SWEEPS + i, x)) * weights

    for r in range(rows):
        part = dot_hot(x[:, 0:NA], mo[:, r * cols : (r + 1) * cols], NN)
        u[:, r, :] = u[:, r, :] + part
    pack(2, lambda m: u[m, 0:rows])
    halo_start(2)
    halo_arrive(2)
    side = halo_fill(2, u)
    for _ in range(SWEEPS):
        side = sweep(side, s_src)

    def out(m, v, rest):
        sol[m] = v
        res[m] = rest

    apply_field(side, rows, out)
    for d, source, target, slot in sent:
        @pl.when(has[d])
        def _():
            copy(source, target, slot, dev[d]).wait_send()

    for k in range(LEVELS):
        mat_copy(k).wait_send()
        vec_copy(k).wait_send()


def shards(n_row, n_col, source, guess, conductivity, storage, aggregates, pair_maps):
    members, rows, cols = source.shape
    cells = rows * cols
    ext = rows + GROUP
    vm = pl.BlockSpec(memory_space=pltpu.VMEM)
    slots = 44 + 4 * NX0 + 2 * LEVELS
    return pl.pallas_call(
        functools.partial(kernel, n_row, n_col),
        out_shape=(jax.ShapeDtypeStruct(source.shape, F32),) * 2,
        in_specs=[vm] * 6,
        out_specs=(vm, vm),
        scratch_shapes=[
            pltpu.VMEM((members, ext, cols), F32),
            pltpu.VMEM((members, ext, cols), F32),
            pltpu.VMEM((members, rows, cols), F32),
            pltpu.VMEM((NA, cells), BF16),
            pltpu.VMEM((3 * NA, cells), BF16),
            pltpu.VMEM((3 * members, cells), BF16),
            pltpu.VMEM((cols, cols), F32),
            pltpu.VMEM((4, rows, cols), F32),
            pltpu.VMEM((4, rows, cols), F32),
            pltpu.VMEM((4, GROUP, cols), F32),
            pltpu.VMEM((4, GROUP, cols), F32),
            pltpu.VMEM((4, rows, cols), jnp.int32),
            pltpu.VMEM((3, 2, WIDE * members, cols), F32),
            pltpu.VMEM((3, 2, rows, cols), F32),
            pltpu.VMEM((3, 4, GROUP, cols), F32),
            pltpu.VMEM((3, 2, WIDE * members, cols), F32),
            pltpu.VMEM((3, rows, cols), F32),
            pltpu.VMEM((NX0, members, cols), F32),
            pltpu.VMEM((NX0, 4, members, cols), F32),
            pltpu.VMEM((LEVELS + 1, NA, cols), F32),
            pltpu.VMEM((LEVELS, NA, cols), F32),
            pltpu.VMEM((LEVELS + 1, members, cols), F32),
            pltpu.VMEM((LEVELS, members, cols), F32),
            pltpu.VMEM((2, 5 * cols, cols), BF16),
            pltpu.VMEM((LEVELS - 1, 4, cols, cols), BF16),
            pltpu.VMEM((LEVELS, cols, cols), BF16),
            pltpu.SemaphoreType.DMA((slots,)),
            pltpu.SemaphoreType.DMA((slots,)),
        ],
        compiler_params=pltpu.CompilerParams(collective_id=0, has_side_effects=True),
    )(source, guess, conductivity, storage, aggregates, pair_maps.reshape(LEVELS, -1))


def solution(mesh):
    placed = (
        P(None, "row", "col"),
        P(None, "row", "col"),
        P("row", "col"),
        P("row", "col"),
        P("row", "col"),
        P(None, "row", "col", None),
    )
    return jax.shard_map(
        functools.partial(shards, mesh.shape["row"], mesh.shape["col"]),
        mesh=mesh,
        in_specs=placed,
        out_specs=(P(None, "row", "col"), P(None, "row", "col")),
        check_vma=False,
    )
```

```python
import functools

import jax
import jax.numpy as jnp
from jax import lax
from jax.experimental import pallas as pl
from jax.experimental.pallas import tpu as pltpu
from jax.sharding import PartitionSpec as P

NA = 64
SWEEPS = 3
LEVELS = 4
OMEGA_FINE = 0.8
OMEGA_COARSE = 0.6
F32 = jnp.float32
BF16 = jnp.bfloat16
MESH = pl.DeviceIdType.MESH
OPP = (1, 0, 3, 2, 7, 6, 5, 4)
WIDE = SWEEPS + 1
GROUP = 2 * WIDE
NX0 = 2 * SWEEPS
NN = (((1,), (0,)), ((), ()))
NT = (((1,), (1,)), ((), ()))


def dg(a, b, dims):
    return lax.dot_general(a, b, dims, preferred_element_type=F32)


def split2(x):
    hi = x.astype(BF16)
    return hi, (x - hi.astype(F32)).astype(BF16)


def split3(x):
    hi = x.astype(BF16)
    rest = x - hi.astype(F32)
    mid = rest.astype(BF16)
    return hi, mid, (rest - mid.astype(F32)).astype(BF16)


def dot_parts(x, w_hi, w_lo, dims=NN):
    hi, lo = split2(x)
    return dg(hi, w_hi, dims) + (dg(lo, w_hi, dims) + dg(hi, w_lo, dims))


def dot_hot(x, hot, dims):
    hi, mid, lo = split3(x)
    return dg(hi, hot, dims) + (dg(mid, hot, dims) + dg(lo, hot, dims))


def hot_dot(hot, x, dims):
    hi, mid, lo = split3(x)
    return dg(hot, hi, dims) + (dg(hot, mid, dims) + dg(hot, lo, dims))


def kernel(n_row, n_col, src, guess, cond, sto, agg, pm, sol, res,
           u, se, left, mo, gmat, rlhs, xt, crecv, srecv, ccorn, scorn, arecv, rowbuf, colbuf, corner,
           rsend, csend, xsend, xrecv, msend, mrecv, vsend, vrecv, wmat, bsp, qts, ssem, rsem):
    members, rows, cols = guess.shape
    ext = rows + GROUP
    row = lax.axis_index("row")
    col = lax.axis_index("col")
    has = [row > 0, row < n_row - 1, col > 0, col < n_col - 1]
    dev = [(row - 1, col), (row + 1, col), (row, col - 1), (row, col + 1)]
    for v in (0, 1):
        for h in (2, 3):
            has.append(jnp.logical_and(has[v], has[h]))
            dev.append((dev[v][0], dev[h][1]))
    col_bit = col % 2
    row_bit = row % 2
    col_bit2 = col // 2 % 2
    row_bit2 = row // 2 % 2
    upper = (col_bit, row_bit, col_bit2, row_bit2)
    partner = (
        (row, col + 1 - 2 * col_bit),
        (row + 1 - 2 * row_bit, col),
        (row, col + 2 - 4 * col_bit2),
        (row + 2 - 4 * row_bit2, col),
    )

    barrier = pltpu.get_barrier_semaphore()
    count = jnp.int32(2)
    for d in range(8):
        count = count + has[d].astype(jnp.int32)

        @pl.when(has[d])
        def _():
            pl.semaphore_signal(barrier, inc=1, device_id=dev[d], device_id_type=MESH)

    for k in (2, 3):
        pl.semaphore_signal(barrier, inc=1, device_id=partner[k], device_id_type=MESH)

    def copy(source, target, slot, device):
        return pltpu.make_async_remote_copy(
            src_ref=source, dst_ref=target, send_sem=ssem.at[slot], recv_sem=rsem.at[slot],
            device_id=device, device_id_type=MESH)

    sent = []

    def start(d, source, target, slot):
        @pl.when(has[d])
        def _():
            copy(source, target, slot, dev[d]).start()

        sent.append((d, source, target, slot))

    def arrive(d, source, target, slot):
        @pl.when(has[OPP[d]])
        def _():
            copy(source, target, slot, dev[d]).wait_recv()

    for d in range(8):
        @pl.when(jnp.logical_not(has[OPP[d]]))
        def _():
            for got, got_corner in ((crecv, ccorn), (srecv, scorn)):
                if d < 4:
                    got[d] = jnp.ones((rows, cols), F32)
                else:
                    got_corner[d - 4] = jnp.ones((GROUP, cols), F32)
            if d < 4:
                arecv[d] = jnp.zeros((rows, cols), jnp.int32)
                for e in range(NX0):
                    xrecv[e, d] = jnp.zeros((members, cols), F32)
            for p in range(3):
                if d < 2:
                    rowbuf[p, d] = jnp.zeros((WIDE * members, cols), F32)
                elif d < 4:
                    colbuf[p, d - 2] = jnp.zeros((rows, cols), F32)
                else:
                    corner[p, d - 4] = jnp.zeros((GROUP, cols), F32)

    lane = lax.broadcasted_iota(jnp.int32, (ext, cols), 1)
    sub = lax.broadcasted_iota(jnp.int32, (ext, cols), 0)
    l8 = lane % GROUP
    owner = lane // GROUP
    lane8 = lane[0:GROUP]
    sub8 = sub[0:GROUP]

    def mirror(x):
        where = lax.broadcasted_iota(jnp.int32, x.shape, 1)
        bit = 1
        while bit < GROUP:
            x = jnp.where(where // bit % 2 == 0, pltpu.roll(x, cols - bit, 1), pltpu.roll(x, bit, 1))
            bit *= 2
        return x

    def repeat(x):
        width = GROUP
        while width < cols:
            x = x + pltpu.roll(x, width, 1)
            width *= 2
        return x

    def halo_ref(p, d):
        source = rsend.at[p, d] if d < 2 else csend.at[p] if d < 4 else csend.at[
            p, pl.ds(0 if d < 6 else rows - GROUP, GROUP)]
        target = rowbuf.at[p, d] if d < 2 else colbuf.at[p, d - 2] if d < 4 else corner.at[p, d - 4]
        return d, source, target, 20 + 8 * p + d

    def part_ref(value, plane, corners, d, slot):
        if d in (2, 3):
            return d, value, plane.at[d], slot
        source = value.at[pl.ds(0 if d in (0, 4, 5) else rows - GROUP, GROUP)]
        target = plane.at[d, pl.ds(0, GROUP)] if d < 2 else corners.at[d - 4]
        return d, source, target, slot

    def pack(p, field_of):
        packed = jnp.zeros((rows, cols), F32)
        for m in range(members):
            v = field_of(m)
            packed = jnp.where(owner[0:rows] == m, pltpu.roll(v, (GROUP * m + WIDE) % cols, 1), packed)
            rsend[p, 0, WIDE * m : WIDE * (m + 1), :] = v[0:WIDE]
            rsend[p, 1, WIDE * m : WIDE * (m + 1), :] = v[rows - WIDE : rows]
        csend[p] = mirror(packed)

    order = (2, 3, 4, 5, 6, 7, 0, 1)

    def halo_start(p):
        for d in order:
            start(*halo_ref(p, d))

    def halo_arrive(p):
        for d in range(8):
            arrive(*halo_ref(p, d))

    def under(south, north):
        return jnp.where(sub8 < WIDE, south, north)

    def halo_fill(p, field):
        for m in range(members):
            field[m, rows : rows + WIDE, :] = rowbuf[p, 0, WIDE * m : WIDE * (m + 1), :]
            field[m, rows + WIDE : ext, :] = rowbuf[p, 1, WIDE * m : WIDE * (m + 1), :]
        side_e = jnp.concatenate([colbuf[p, 0], under(corner[p, 0], corner[p, 2])], axis=0)
        side_w = jnp.concatenate([colbuf[p, 1], under(corner[p, 1], corner[p, 3])], axis=0)
        return jnp.where(l8 < WIDE, side_e, side_w)

    def cond_parts(d):
        return part_ref(cond, crecv, ccorn, d, d)

    def sto_parts(d):
        return part_ref(sto, srecv, scorn, d, 8 + d)

    pack(0, lambda m: guess[m])
    pack(1, lambda m: src[m])
    pl.semaphore_wait(barrier, count)
    for d in order:
        start(*cond_parts(d))
    for d in range(4):
        start(d, agg, arecv.at[d], 16 + d)
    for d in order:
        start(*sto_parts(d))
    halo_start(0)
    halo_start(1)

    agg_v = agg[...]
    sub64 = lax.broadcasted_iota(jnp.int32, (NA, cols), 0)
    for r in range(rows):
        mo[:, r * cols : (r + 1) * cols] = jnp.where(
            sub64 == agg_v[r : r + 1], 1.0, 0.0).astype(BF16)
    wmat[...] = jnp.zeros(wmat.shape, BF16)
    msend[...] = jnp.zeros(msend.shape, F32)
    xt[...] = jnp.zeros(xt.shape, F32)
    iota128 = lax.broadcasted_iota(jnp.int32, (cols, cols), 0)
    for k in range(LEVELS):
        pmk = pm[k : k + 1, :]
        pmk = jnp.where(upper[k] == 1, pltpu.roll(pmk, NA, 1), pmk)
        qts[k] = jnp.where(iota128 == pmk, 1.0, 0.0).astype(BF16)

    def face(a, b):
        return 2.0 * (a * b) / (a + b)

    last = rows - 1
    c = cond[...]
    in_east = jnp.where(lane[0:rows] < cols - 1, face(c, pltpu.roll(c, cols - 1, 1)), 0.0)
    in_south = jnp.where(sub[0:rows] < last, face(c, pltpu.roll(c, last, 0)), 0.0)
    right = pltpu.roll(agg_v, cols - 1, 1)
    below = pltpu.roll(agg_v, last, 0)
    half = 0.5 * (sto[...] + in_east + pltpu.roll(in_east, 1, 1) + in_south + pltpu.roll(in_south, 1, 0))
    for r in range(rows):
        s = slice(r, r + 1)
        g = (jnp.where(sub64 == right[s], in_east[s], 0.0)
             + jnp.where(sub64 == below[s], in_south[s], 0.0)
             - jnp.where(sub64 == agg_v[s], half[s], 0.0))
        for i, part in enumerate(split3(g)):
            gmat[i * NA : (i + 1) * NA, r * cols : (r + 1) * cols] = part
    gx = dg(gmat[...], mo[...], NT)
    xt[0:NA, 0:NA] = gx[0:NA] + (gx[NA : 2 * NA] + gx[2 * NA : 3 * NA])
    xfull = xt[...]
    inner = -(xfull + xfull.T)[0:NA]

    for d in range(8):
        arrive(*cond_parts(d))
        arrive(*sto_parts(d))

    def extend(value, plane, corners):
        main = jnp.concatenate([value[...], under(plane[0, 0:GROUP], plane[1, 0:GROUP])], axis=0)
        side_e = jnp.concatenate([plane[2], under(corners[0], corners[2])], axis=0)
        side_w = jnp.concatenate([plane[3], under(corners[1], corners[3])], axis=0)
        base = jnp.where(lane < WIDE, pltpu.roll(side_w, WIDE, 1), pltpu.roll(side_e, WIDE, 1))
        side = mirror(repeat(jnp.where(lane < GROUP, base, 0.0)))
        return main, side

    cm, cs = extend(cond, crecv, ccorn)
    sm, ss = extend(sto, srecv, scorn)
    hasi = [h.astype(jnp.int32) for h in has[0:4]]

    def vertical(x):
        down = jnp.where(jnp.logical_and(sub == last, hasi[1] == 0), 0.0, face(x, pltpu.roll(x, ext - 1, 0)))
        up = jnp.where(jnp.logical_and(sub == 0, hasi[0] == 0), 0.0, face(x, pltpu.roll(x, 1, 0)))
        return down, up

    side_at = pltpu.roll(cs, cols - WIDE, 1)
    rim = jnp.logical_and(lane >= WIDE - 1, lane <= WIDE)
    main_at = repeat(jnp.where(rim, pltpu.roll(cm, WIDE, 1), 0.0))
    east = face(cm, jnp.where(lane == cols - 1, side_at, pltpu.roll(cm, cols - 1, 1)))
    west = face(cm, jnp.where(lane == 0, side_at, pltpu.roll(cm, 1, 1)))
    east = jnp.where(lane < cols - 1 + hasi[3], east, 0.0)
    west = jnp.where(lane >= 1 - hasi[2], west, 0.0)
    south, north = vertical(cm)
    diag = sm + east + west + south + north
    step = OMEGA_FINE / diag
    s_west = face(cs, jnp.where(l8 == WIDE - 1, main_at, pltpu.roll(cs, cols - 1, 1)))
    s_east = face(cs, jnp.where(l8 == WIDE, main_at, pltpu.roll(cs, 1, 1)))
    s_west = jnp.where(jnp.logical_and(l8 == WIDE - 1, hasi[3] == 0), 0.0, s_west)
    s_east = jnp.where(jnp.logical_and(l8 == WIDE, hasi[2] == 0), 0.0, s_east)
    s_south, s_north = vertical(cs)
    s_diag = ss + s_east + s_west + s_south + s_north
    s_step = OMEGA_FINE / s_diag

    def apply_field(side, n, finish):
        lane_n = lane[0:n]
        edge = jnp.zeros((ext, cols), F32)
        for m in range(members):
            v = u[m]
            hm = pltpu.roll(side, (2 * cols - GROUP * m - WIDE) % cols, 1)[0:n]
            vn = v[0:n]
            from_w = jnp.where(lane_n == 0, hm, pltpu.roll(vn, 1, 1))
            from_e = jnp.where(lane_n == cols - 1, hm, pltpu.roll(vn, cols - 1, 1))
            from_s = pltpu.roll(v, ext - 1, 0)[0:n]
            from_n = pltpu.roll(v, 1, 0)[0:n]
            rest = se[m, 0:n] - (diag[0:n] * vn - (
                east[0:n] * from_e + west[0:n] * from_w + south[0:n] * from_s + north[0:n] * from_n))
            if n == ext:
                edge = jnp.where(owner == m, pltpu.roll(v, (GROUP * m + WIDE) % cols, 1), edge)
            finish(m, vn, rest)
        return edge

    def sweep(side, s_src):
        def finish(m, v, rest):
            u[m] = v + step * rest

        edge = apply_field(side, ext, finish)
        from_w = jnp.where(l8 == WIDE - 1, edge, pltpu.roll(side, cols - 1, 1))
        from_e = jnp.where(l8 == WIDE, edge, pltpu.roll(side, 1, 1))
        rest = s_src - (s_diag * side - (s_east * from_e + s_west * from_w
                        + s_south * pltpu.roll(side, ext - 1, 0) + s_north * pltpu.roll(side, 1, 0)))
        return side + s_step * rest


    for d in range(4):
        arrive(d, agg, arecv.at[d], 16 + d)
    agg_t = agg_v.astype(F32).T.astype(jnp.int32)

    def couple(slot, own_ids, other_ids, faces, width):
        own = jnp.where(lax.broadcasted_iota(jnp.int32, (cols, width), 0) == own_ids, 1.0, 0.0).astype(BF16)
        other = jnp.where(lax.broadcasted_iota(jnp.int32, (NA, width), 0) == other_ids, faces, 0.0)
        links = dot_hot(other, own, NT)
        hi, lo = split2(-links)
        wmat[0, slot * cols : slot * cols + NA] = hi
        wmat[1, slot * cols : slot * cols + NA] = lo
        return jnp.sum(links, axis=0, keepdims=True)

    outer = couple(1, agg_v[last:rows], arecv[0][0:1], south[last:rows], cols)
    outer = outer + couple(2, agg_v[0:1], arecv[1][last : rows], north[0:1], cols)
    agg_e = arecv[2].astype(F32).T.astype(jnp.int32)
    agg_w = arecv[3].astype(F32).T.astype(jnp.int32)
    outer = outer + couple(3, agg_t[cols - 1 : cols], agg_e[0:1], east[0:rows].T[cols - 1 : cols], rows)
    outer = outer + couple(4, agg_t[0:1], agg_w[cols - 1 : cols], west[0:rows].T[0:1], rows)
    def mat_copy(k):
        return copy(msend.at[k], mrecv.at[k], 44 + 4 * NX0 + k, partner[k])

    def vec_copy(k):
        return copy(vsend.at[k], vrecv.at[k], 44 + 4 * NX0 + LEVELS + k, partner[k])

    lane_c = lax.broadcasted_iota(jnp.int32, (NA, cols), 1)
    lane_1 = lax.broadcasted_iota(jnp.int32, (1, cols), 1)

    def weight(mat):
        d = jnp.sum(jnp.where(lane_c == sub64, mat, 0.0), axis=0, keepdims=True)
        ok = lane_1 < NA
        return jnp.where(ok, OMEGA_COARSE / jnp.where(ok, d, 1.0), 0.0)

    def next_mat(k):
        mat_copy(k).wait_recv()
        both = jnp.concatenate([msend[k], pltpu.roll(mrecv[k], NA, 1)], axis=0)
        qt = qts[k]
        mat = hot_dot(qt[0:NA], dot_hot(both, qt, NT), NN)
        msend[k + 1] = mat
        if k + 1 < LEVELS:
            mat_copy(k + 1).start()
            eye = jnp.where(lane_c == sub64, 1.0, 0.0)
            side_w = OMEGA_COARSE / jnp.sum(eye * mat, axis=1, keepdims=True)
            one = eye - mat * weight(mat)
            hi, lo = split2(one)
            two = dot_parts(one[:, 0:NA], hi, lo)
            parts = split2(dot_parts(two[:, 0:NA], hi, lo)) + split2(side_w * (eye + one + two))
            for i in range(4):
                bsp[k, i, 0:NA] = parts[i]
                if i < 2:
                    bsp[k, i, NA:cols] = jnp.zeros((cols - NA, cols), BF16)

    block = inner + jnp.where(lane_c == sub64, outer, 0.0)
    msend[0] = block
    mat_copy(0).start()
    hi, lo = split2(block)
    wmat[0, 0:NA] = hi
    wmat[1, 0:NA] = lo
    weights = weight(block)

    for m in range(members):
        u[m, 0:rows] = guess[m]
        se[m, 0:rows] = src[m]
    halo_arrive(0)
    side = halo_fill(0, u)
    halo_arrive(1)
    s_src = halo_fill(1, se)
    for _ in range(SWEEPS):
        side = sweep(side, s_src)

    def keep_left(m, v, rest):
        left[m] = rest

    apply_field(side, rows, keep_left)
    next_mat(0)
    for r in range(rows):
        for i, part in enumerate(split3(left[:, r, :])):
            rlhs[i * members : (i + 1) * members, r * cols : (r + 1) * cols] = part
    gr = dg(rlhs[...], mo[...], NT)
    vsend[LEVELS] = jnp.zeros((members, cols), F32)
    vsend[LEVELS, :, 0:NA] = gr[0:members] + (gr[members : 2 * members] + gr[2 * members : 3 * members])
    y0 = vsend[LEVELS]

    def x_slot(e, d):
        return (d, xsend.at[e], xrecv.at[e, d], 44 + 4 * e + d)

    def level_one(e, x, between=None):
        xsend[e] = x
        for d in (2, 3, 0, 1):
            start(*x_slot(e, d))
        if between is not None:
            between()
        for d in range(4):
            arrive(*x_slot(e, d))
        every = jnp.concatenate([x] + [xrecv[e, d] for d in range(4)], axis=1)
        return dot_parts(every, wmat[0], wmat[1])

    inverse = []

    def last_mat():
        next_mat(3)
        mat = jnp.where(lane_c < NA, msend[LEVELS], jnp.where(lane_c - NA == sub64, 1.0, 0.0))
        for k in range(NA):
            pivot = mat[k : k + 1] / mat[k : k + 1, k : k + 1]
            mat = jnp.where(sub64 == k, pivot, mat - mat[:, k : k + 1] * pivot)
        inverse.append(jnp.where(lane_c < NA, pltpu.roll(mat, NA, 1), 0.0))

    x = y0 * weights
    x = x + (y0 - level_one(0, x, lambda: next_mat(1))) * weights
    x = x + (y0 - level_one(1, x, lambda: next_mat(2))) * weights
    rem = y0 - level_one(2, x, last_mat)
    sols = [x]
    for k in range(LEVELS):
        vsend[k] = rem
        vec_copy(k).start()
        vec_copy(k).wait_recv()
        y = dot_hot(rem + pltpu.roll(vrecv[k], NA, 1), qts[k], NT)
        if k < LEVELS - 1:
            rem = dot_parts(y, bsp[k, 0], bsp[k, 1], NT)
            x = dot_parts(y[:, 0:NA], bsp[k, 2, 0:NA], bsp[k, 3, 0:NA])
        else:
            x = lax.dot_general(y[:, 0:NA], inverse[0], NN, precision=lax.Precision.HIGHEST,
                                preferred_element_type=F32)
        sols.append(x)
    lane_m = lax.broadcasted_iota(jnp.int32, (members, cols), 1)
    for k in reversed(range(LEVELS)):
        x = sols[k] + jnp.where(lane_m < NA, dot_hot(x, qts[k], NN), 0.0)
        if k > 0:
            x = sols[k] + dot_parts(x[:, 0:NA], bsp[k - 1, 0, 0:NA], bsp[k - 1, 1, 0:NA])
        else:
            for i in range(SWEEPS):
                x = x + (y0 - level_one(SWEEPS + i, x)) * weights

    for r in range(rows):
        part = dot_hot(x[:, 0:NA], mo[:, r * cols : (r + 1) * cols], NN)
        u[:, r, :] = u[:, r, :] + part
    pack(2, lambda m: u[m, 0:rows])
    halo_start(2)
    halo_arrive(2)
    side = halo_fill(2, u)
    for _ in range(SWEEPS):
        side = sweep(side, s_src)

    def out(m, v, rest):
        sol[m] = v
        res[m] = rest

    apply_field(side, rows, out)
    for d, source, target, slot in sent:
        @pl.when(has[d])
        def _():
            copy(source, target, slot, dev[d]).wait_send()

    for k in range(LEVELS):
        mat_copy(k).wait_send()
        vec_copy(k).wait_send()


def shards(n_row, n_col, source, guess, conductivity, storage, aggregates, pair_maps):
    members, rows, cols = source.shape
    cells = rows * cols
    ext = rows + GROUP
    vm = pl.BlockSpec(memory_space=pltpu.VMEM)
    slots = 44 + 4 * NX0 + 2 * LEVELS
    return pl.pallas_call(
        functools.partial(kernel, n_row, n_col),
        out_shape=(jax.ShapeDtypeStruct(source.shape, F32),) * 2,
        in_specs=[vm] * 6,
        out_specs=(vm, vm),
        scratch_shapes=[
            pltpu.VMEM((members, ext, cols), F32),
            pltpu.VMEM((members, ext, cols), F32),
            pltpu.VMEM((members, rows, cols), F32),
            pltpu.VMEM((NA, cells), BF16),
            pltpu.VMEM((3 * NA, cells), BF16),
            pltpu.VMEM((3 * members, cells), BF16),
            pltpu.VMEM((cols, cols), F32),
            pltpu.VMEM((4, rows, cols), F32),
            pltpu.VMEM((4, rows, cols), F32),
            pltpu.VMEM((4, GROUP, cols), F32),
            pltpu.VMEM((4, GROUP, cols), F32),
            pltpu.VMEM((4, rows, cols), jnp.int32),
            pltpu.VMEM((3, 2, WIDE * members, cols), F32),
            pltpu.VMEM((3, 2, rows, cols), F32),
            pltpu.VMEM((3, 4, GROUP, cols), F32),
            pltpu.VMEM((3, 2, WIDE * members, cols), F32),
            pltpu.VMEM((3, rows, cols), F32),
            pltpu.VMEM((NX0, members, cols), F32),
            pltpu.VMEM((NX0, 4, members, cols), F32),
            pltpu.VMEM((LEVELS + 1, NA, cols), F32),
            pltpu.VMEM((LEVELS, NA, cols), F32),
            pltpu.VMEM((LEVELS + 1, members, cols), F32),
            pltpu.VMEM((LEVELS, members, cols), F32),
            pltpu.VMEM((2, 5 * cols, cols), BF16),
            pltpu.VMEM((LEVELS - 1, 4, cols, cols), BF16),
            pltpu.VMEM((LEVELS, cols, cols), BF16),
            pltpu.SemaphoreType.DMA((slots,)),
            pltpu.SemaphoreType.DMA((slots,)),
        ],
        compiler_params=pltpu.CompilerParams(collective_id=0, has_side_effects=True),
    )(source, guess, conductivity, storage, aggregates, pair_maps.reshape(LEVELS, -1))


def solution(mesh):
    placed = (
        P(None, "row", "col"),
        P(None, "row", "col"),
        P("row", "col"),
        P("row", "col"),
        P("row", "col"),
        P(None, "row", "col", None),
    )
    return jax.shard_map(
        functools.partial(shards, mesh.shape["row"], mesh.shape["col"]),
        mesh=mesh,
        in_specs=placed,
        out_specs=(P(None, "row", "col"), P(None, "row", "col")),
        check_vma=False,
    )
```
